512 devices in a mesh: ifg: 128 (over x, z, core), tile: 4 (over y).
Axes of the slice: x: 4, y: 4, z: 16, core: 2. Of those that a mesh axis runs over, the one named last changes fastest.
Arguments:
- ifgs: bfloat16 [1152, 8, 16384], P('ifg', 'tile'), may hold values from -12 to 12
- pairs: int32 [1152, 2], replicated, may hold values from 0 to 299, as said below
- pseudo_inverse: bfloat16 [300, 1152], P(None, 'ifg'), may hold values from -0.1875 to 0.1875
- ref_pixels: int32 [64], replicated, may hold values from 0 to 131071
- epochs: int32 [8], replicated, may hold values from 8 to 291
Outputs:
- coefficients: float32 [16, 8, 16384], P(None, 'tile', 'ifg')
- misfit_rms: float32 [8, 16384], P('tile', 'ifg')
The draws below stay inside these ranges and needn't reach their ends.
Inputs may be any that keep to these rules, and one draw needn't show every extreme that they name: pairs[k, 0] < pairs[k, 1] <= pairs[k, 0] + 6.
All inputs are finite; a program needn't handle non-finite values.
Results may differ from the reference program's by a relative error of at most 0.0029.
Values may be sent and summed in bfloat16 or wider, within the bound.
A program may use at most 64 MiB of HBM per device.

```python
import math
import jax
import jax.numpy as jnp
from jax import lax

DATES = 300
PAIRS = 1152
EPOCHS = 8
TERMS = 16
REF = 64
COL_DEV = 128
ROWS = 8
COLS = 16384
N_IFG = 128


def draw_pairs(key, part):
    first_key = jax.random.fold_in(key, 11)
    gap_key = jax.random.fold_in(key, 23)
    first = jax.random.randint(first_key, (PAIRS,), 0, DATES - 1, dtype=jnp.int32)
    gap = jax.random.randint(gap_key, (PAIRS,), 1, 7, dtype=jnp.int32)
    second = jnp.minimum(first + gap, DATES - 1)
    return jnp.stack([first, second], axis=1)


def with_ends(drawn, stream_key, low, largest):
    place = [jax.random.randint(jax.random.fold_in(stream_key, axis), (), 0, length) for axis, length in enumerate(drawn.shape)]
    main_axis = drawn.shape.index(max(drawn.shape))
    neighbour = place[:main_axis] + [(place[main_axis] + 1) % drawn.shape[main_axis]] + place[main_axis + 1:]
    return drawn.at[tuple(place)].set(low).at[tuple(neighbour)].set(largest)


def level_of(own_key, dims, cuts, smallest, high):
    factor_of, own = 1.0, jax.random.fold_in(own_key, 6)
    for position, parts in cuts:
        heights = jnp.exp(jax.random.uniform(jax.random.fold_in(own, position), (parts,), jnp.float32, smallest / len(cuts), high / len(cuts)))
        factor_of = factor_of * jnp.repeat(heights, dims[position] // parts).reshape([-1 if axis == position else 1 for axis in range(len(dims))])
    return factor_of


def bell_draw(stream_key, dims, scale, bound, split=(), held_as=jnp.bfloat16):
    array = jax.random.normal(stream_key, dims, jnp.float32) * scale
    if len(split) > 0:
        array = level_of(stream_key, dims, split, -0.22, 0.18) * array
    return jnp.clip(array, min=-bound, max=bound).astype(held_as)


def setup_inputs(seed: int = 0) -> dict:
    seeds = jax.random.split(jax.random.key(seed), 6)
    ifgs = bell_draw(seeds[0], (PAIRS, ROWS, COLS), 2.0, 12.0, ((0, 128), (1, 4)))
    pairs = draw_pairs(jax.random.fold_in(seeds[5], 71), 0)
    pseudo_inverse = bell_draw(seeds[2], (DATES, PAIRS), PAIRS ** -0.5, 0.1875, ((1, 128),))
    ref_pixels = with_ends(jax.random.randint(seeds[3], (REF,), 0, ROWS * COLS), jax.random.fold_in(seeds[3], 1), 0, (ROWS * COLS) - 1).astype(jnp.int32)
    epochs = with_ends(jax.random.randint(seeds[4], (EPOCHS,), 8, DATES - 8), jax.random.fold_in(seeds[4], 1), 8, (DATES - 8) - 1).astype(jnp.int32)
    return dict(ifgs=ifgs, pairs=pairs, pseudo_inverse=pseudo_inverse, ref_pixels=ref_pixels, epochs=epochs)


EPS = 1e-06
RIDGE = 1.0

def design(epochs, count):
    index = jnp.arange(count, dtype=jnp.int32)
    days = index.astype(jnp.float32)
    scaled = 2.0 * days / (count - 1) - 1.0
    years = days * 12.0 / 365.25
    smooth = jnp.stack([jnp.ones_like(days), scaled, scaled * scaled, scaled * scaled * scaled, jnp.sin(2.0 * math.pi * years), jnp.cos(2.0 * math.pi * years), jnp.sin(4.0 * math.pi * years), jnp.cos(4.0 * math.pi * years)], axis=1)
    jumps = (index[:, None] >= epochs[None, :]).astype(jnp.float32)
    return jnp.concatenate([smooth, jumps], axis=1)

def fit_operator(epochs, count):
    matrix = design(epochs, count)
    normal = jnp.dot(matrix.T.astype(jnp.float32), matrix.astype(jnp.float32), precision=lax.Precision.HIGHEST, preferred_element_type=jnp.float32)
    normal = normal + RIDGE * jnp.eye(matrix.shape[1], dtype=jnp.float32)
    return jnp.linalg.solve(normal, matrix.T)

def incidence_matrix(pairs, count):
    dates = jnp.arange(count, dtype=jnp.int32)
    later = (pairs[:, 1:2] == dates[None, :]).astype(jnp.float32)
    earlier = (pairs[:, 0:1] == dates[None, :]).astype(jnp.float32)
    return later - earlier

def reference(ifgs, pairs, pseudo_inverse, ref_pixels, epochs):
    flat_view = ifgs.reshape(PAIRS, ROWS * COLS)
    region = jnp.take(flat_view, ref_pixels, axis=1).astype(jnp.float32)
    means = lax.optimization_barrier(jnp.sum(region, axis=1)) / REF
    operator = fit_operator(epochs, DATES)
    incidence = incidence_matrix(pairs, DATES)

    def block(index):
        piece = lax.dynamic_slice_in_dim(ifgs, index * COL_DEV, COL_DEV, 2)
        corrected = (piece.astype(jnp.float32) - means[:, None, None]).astype(jnp.bfloat16).reshape(PAIRS, ROWS * COL_DEV)
        displacement = jnp.dot(pseudo_inverse.astype(jnp.float32), corrected.astype(jnp.float32), preferred_element_type=jnp.float32)
        coeffs = jnp.dot(operator.astype(jnp.float32), displacement.astype(jnp.float32), precision=lax.Precision.HIGHEST, preferred_element_type=jnp.float32)
        predicted = jnp.dot(incidence.astype(jnp.float32), displacement.astype(jnp.float32), precision=lax.Precision.HIGHEST, preferred_element_type=jnp.float32)
        misfit = corrected.astype(jnp.float32) - predicted
        spread = jnp.sqrt(lax.optimization_barrier(jnp.mean(misfit * misfit, axis=0)) + EPS)
        return (coeffs.reshape(TERMS, ROWS, COL_DEV), spread.reshape(ROWS, COL_DEV))
    coeff_blocks, spread_blocks = lax.map(block, jnp.arange(N_IFG, dtype=jnp.int32))
    coefficients = jnp.transpose(coeff_blocks, (1, 2, 0, 3)).reshape(TERMS, ROWS, COLS)
    misfit_rms = jnp.transpose(spread_blocks, (1, 0, 2)).reshape(ROWS, COLS)
    return (coefficients, misfit_rms)
```

```python
import functools
import math

import jax
import jax.numpy as jnp
from jax import lax
from jax.experimental import pallas as pl
from jax.experimental.pallas import tpu as pltpu
from jax.sharding import PartitionSpec as P

EPS = 1e-06
RIDGE = 1.0


def design(epochs, count):
    index = jnp.arange(count, dtype=jnp.int32)
    days = index.astype(jnp.float32)
    scaled = 2.0 * days / (count - 1) - 1.0
    years = days * 12.0 / 365.25
    smooth = jnp.stack(
        [
            jnp.ones_like(days),
            scaled,
            scaled * scaled,
            scaled * scaled * scaled,
            jnp.sin(2.0 * math.pi * years),
            jnp.cos(2.0 * math.pi * years),
            jnp.sin(4.0 * math.pi * years),
            jnp.cos(4.0 * math.pi * years),
        ],
        axis=1,
    )
    jumps = (index[:, None] >= epochs[None, :]).astype(jnp.float32)
    return jnp.concatenate([smooth, jumps], axis=1)


def fit_operator(epochs, count):
    matrix = design(epochs, count)
    normal = jnp.dot(
        matrix.T, matrix, precision=lax.Precision.HIGHEST, preferred_element_type=jnp.float32
    )
    normal = normal + RIDGE * jnp.eye(matrix.shape[1], dtype=jnp.float32)
    factor = jnp.linalg.cholesky(normal)
    return jax.scipy.linalg.cho_solve((factor, True), matrix.T)


def incidence_matrix(pairs, count):
    dates = jnp.arange(count, dtype=jnp.int32)
    later = (pairs[:, 1:2] == dates[None, :]).astype(jnp.float32)
    earlier = (pairs[:, 0:1] == dates[None, :]).astype(jnp.float32)
    return later - earlier


MESH = pl.DeviceIdType.MESH
LANES = 128


def reference_sums(region, ifgs, out):
    count, rows, width = ifgs.shape
    lane = lax.broadcasted_iota(jnp.int32, out.shape, 2)
    row = lax.broadcasted_iota(jnp.int32, out.shape, 1) + lax.axis_index("tile") * rows

    def collect(i, total):
        pixel = region[i]
        col = lax.rem(pixel, width)
        block = lax.div(col, LANES) * LANES
        values = ifgs[:, :, pl.ds(pl.multiple_of(block, LANES), LANES)].astype(jnp.float32)
        hit = (lane == lax.rem(col, LANES)) & (row == lax.div(pixel, width))
        return total + jnp.where(hit, values, 0.0)

    out[...] = lax.fori_loop(0, region.shape[0], collect, jnp.zeros(out.shape, jnp.float32))


def exchange(dims, ifgs, inverse, local, moved, gathered, sent, sums, sem):
    nx, nz, nc, tiles, region_size = dims
    group = nx * nz * nc
    half = nz // 2
    tile = lax.axis_index("tile")
    me = lax.axis_index("ifg")
    my_c = lax.rem(me, nc)
    my_z = lax.rem(lax.div(me, nc), nz)
    my_x = lax.div(me, nc * nz)

    def place(step):
        plane = lax.div(step, nx * nc)
        inner = lax.rem(step, nx * nc)
        j = lax.div(plane + 1, 2)
        odd = lax.rem(plane, 2)
        dz = odd * (half - j) + (1 - odd) * (half + j)
        dx = nx - 1 - lax.div(inner, nc)
        dc = nc - 1 - lax.rem(inner, nc)
        return lax.rem(my_x + dx, nx), lax.rem(my_z + dz, nz), lax.rem(my_c + dc, nc)

    def device(x, z, c):
        return {"ifg": (x * nz + z) * nc + c, "tile": tile}

    barrier = pltpu.get_barrier_semaphore()

    def greet(step, carry):
        pl.semaphore_signal(
            barrier, inc=1, device_id=device(*place(step)), device_id_type=MESH
        )
        return carry

    lax.fori_loop(0, group - 1, greet, 0)
    for d in range(1, tiles):
        pl.semaphore_signal(
            barrier,
            inc=1,
            device_id={"ifg": me, "tile": lax.rem(tile + d, tiles)},
            device_id_type=MESH,
        )

    own = pltpu.make_async_copy(inverse, gathered.at[my_c, my_x, my_z], sem.at[0])
    own.start()

    count, rows, _ = ifgs.shape
    pl.semaphore_wait(barrier, group - 1 + tiles - 1)

    def partial_copy(d):
        return pltpu.make_async_remote_copy(
            src_ref=local,
            dst_ref=sums.at[d - 1],
            send_sem=sem.at[d],
            recv_sem=sem.at[tiles + d],
            device_id={"ifg": me, "tile": lax.rem(tile + d, tiles)},
            device_id_type=MESH,
        )

    for d in range(1, tiles):
        partial_copy(d).start()

    base = 2 * tiles

    def z_copy(dz, ref):
        return pltpu.make_async_remote_copy(
            src_ref=ref,
            dst_ref=gathered.at[my_c, my_x, my_z],
            send_sem=sem.at[base],
            recv_sem=sem.at[base + 1],
            device_id=device(my_x, lax.rem(my_z + dz, nz), my_c),
            device_id_type=MESH,
        )

    def send_z(i, carry):
        j = lax.div(i + 1, 2)
        odd = lax.rem(i, 2)
        z_copy(odd * (half - j) + (1 - odd) * (half + j), inverse).start()
        return carry

    lax.fori_loop(0, nz - 1, send_z, 0)

    for d in range(1, tiles):
        partial_copy(d).wait()
    total = local[...]
    for d in range(1, tiles):
        total = total + sums[d - 1]
    mean = jnp.sum(total, axis=(1, 2), keepdims=True) / region_size
    mean = jnp.broadcast_to(mean, (count, rows, LANES))

    def corrected(x, z, c):
        col = ((x * nz + z) * nc + c) * LANES
        values = ifgs[:, :, pl.ds(pl.multiple_of(col, LANES), LANES)].astype(jnp.float32)
        return (values - mean).astype(jnp.bfloat16)

    def prepare(step, carry):
        sent[step] = corrected(*place(step))
        return carry

    def block_copy(step):
        return pltpu.make_async_remote_copy(
            src_ref=sent.at[step],
            dst_ref=moved.at[my_c, my_x, my_z],
            send_sem=sem.at[base + 2],
            recv_sem=sem.at[base + 3],
            device_id=device(*place(step)),
            device_id_type=MESH,
        )

    def send_block(step, carry):
        block_copy(step).start()
        return carry

    plane = nx * nc
    first = plane * 5
    lax.fori_loop(0, plane, prepare, 0)

    def both(step, carry):
        send_block(step, carry)
        return prepare(step + plane, carry)

    lax.fori_loop(0, first, both, 0)

    own.wait()
    arrived = pltpu.make_async_remote_copy(
        src_ref=gathered.at[0, 0, pl.ds(0, nz - 1)],
        dst_ref=gathered.at[0, 0, pl.ds(0, nz - 1)],
        send_sem=sem.at[base],
        recv_sem=sem.at[base + 1],
        device_id=device(my_x, lax.rem(my_z + 1, nz), my_c),
        device_id_type=MESH,
    )
    arrived.wait()

    def x_copy(d):
        return pltpu.make_async_remote_copy(
            src_ref=gathered.at[my_c, my_x],
            dst_ref=gathered.at[my_c, my_x],
            send_sem=sem.at[base + 3 + 2 * d],
            recv_sem=sem.at[base + 4 + 2 * d],
            device_id=device(lax.rem(my_x + d, nx), my_z, my_c),
            device_id_type=MESH,
        )

    for d in range(1, nx):
        x_copy(d).start()

    lax.fori_loop(first, group - 1 - plane, both, 0)
    lax.fori_loop(group - 1 - plane, group - 1, send_block, 0)
    moved[my_c, my_x, my_z] = corrected(my_x, my_z, my_c)

    for d in range(1, nx):
        x_copy(d).wait()
    core = pltpu.make_async_remote_copy(
        src_ref=gathered.at[my_c],
        dst_ref=gathered.at[my_c],
        send_sem=sem.at[base + 5 + 2 * nx],
        recv_sem=sem.at[base + 6 + 2 * nx],
        device_id=device(my_x, my_z, lax.rem(my_c + 1, nc)),
        device_id_type=MESH,
    )
    core.start()
    everything = pltpu.make_async_remote_copy(
        src_ref=sent.at[pl.ds(0, group - 1)],
        dst_ref=sent.at[pl.ds(0, group - 1)],
        send_sem=sem.at[base + 2],
        recv_sem=sem.at[base + 3],
        device_id=device(my_x, lax.rem(my_z + 1, nz), my_c),
        device_id_type=MESH,
    )
    everything.wait()
    core.wait()


def shards(ifgs, pairs, pseudo_inverse, ref_pixels, epochs, physical):
    nx, nz, nc = physical
    count, row_count, _ = ifgs.shape
    group = lax.axis_size("ifg")
    tiles = lax.axis_size("tile")
    date_count = pseudo_inverse.shape[0]
    padded = -(-date_count // LANES) * LANES
    pairs_up = -(-count // 2)
    inverse = jnp.pad(
        pseudo_inverse.T, ((0, 2 * pairs_up - count), (0, padded - date_count))
    ).reshape(pairs_up, 2, padded)
    vmem = pl.BlockSpec(memory_space=pltpu.VMEM)
    local = pl.pallas_call(
        reference_sums,
        out_shape=jax.ShapeDtypeStruct((count, row_count, LANES), jnp.float32),
        in_specs=[pl.BlockSpec(memory_space=pltpu.SMEM), vmem],
        out_specs=vmem,
    )(ref_pixels, ifgs)
    moved, gathered = pl.pallas_call(
        functools.partial(exchange, (nx, nz, nc, tiles, ref_pixels.shape[0])),
        out_shape=(
            jax.ShapeDtypeStruct((nc, nx, nz, count, row_count, LANES), jnp.bfloat16),
            jax.ShapeDtypeStruct((nc, nx, nz, pairs_up, 2, padded), jnp.bfloat16),
        ),
        in_specs=[vmem, vmem, vmem],
        out_specs=(vmem, vmem),
        scratch_shapes=[
            pltpu.VMEM((group, count, row_count, LANES), jnp.bfloat16),
            pltpu.VMEM((tiles - 1, count, row_count, LANES), jnp.float32),
            pltpu.SemaphoreType.DMA((2 * tiles + 7 + 2 * nx,)),
        ],
        compiler_params=pltpu.CompilerParams(collective_id=0, has_side_effects=True),
    )(ifgs, inverse, local)
    total = group * count
    pixel_rows = moved.reshape(total, row_count * LANES)
    operator = gathered.reshape(group, 2 * pairs_up, padded)[:, :count, :date_count]
    displacement = lax.dot_general(
        operator.reshape(total, date_count),
        pixel_rows,
        (((0,), (0,)), ((), ())),
        preferred_element_type=jnp.float32,
    )
    fit = fit_operator(epochs, date_count)
    coeffs = jnp.dot(
        fit, displacement, precision=lax.Precision.HIGHEST, preferred_element_type=jnp.float32
    )
    ordered = pairs.reshape(nx, nz, nc, count, 2).transpose(2, 0, 1, 3, 4).reshape(total, 2)
    incidence = incidence_matrix(ordered, date_count)
    predicted = jnp.dot(
        incidence, displacement, precision=lax.Precision.HIGHEST, preferred_element_type=jnp.float32
    )
    misfit = pixel_rows.astype(jnp.float32) - predicted
    spread = jnp.sqrt(jnp.mean(misfit * misfit, axis=0) + EPS)
    return (
        coeffs.reshape(fit.shape[0], row_count, LANES),
        spread.reshape(row_count, LANES),
    )


def solution(mesh):
    nx, nc = 4, 2
    nz = mesh.shape["ifg"] // (nx * nc)
    in_specs = (P("ifg", "tile", None), P(), P(None, "ifg"), P(), P())
    out_specs = (P(None, "tile", "ifg"), P("tile", "ifg"))
    run = functools.partial(shards, physical=(nx, nz, nc))
    return jax.shard_map(run, mesh=mesh, in_specs=in_specs, out_specs=out_specs, check_vma=False)
```

```python
import functools

import jax
import jax.numpy as jnp
import numpy as np
from jax import lax
from jax.experimental import pallas as pl
from jax.experimental.pallas import tpu as pltpu
from jax.sharding import PartitionSpec as P

EPS = 1e-06
RIDGE = 1.0


def smooth_columns(count, padded):
    days = np.arange(count, dtype=np.float64)
    scaled = 2.0 * days / (count - 1) - 1.0
    years = days * 12.0 / 365.25
    smooth = np.stack(
        [
            np.ones_like(days),
            scaled,
            scaled**2,
            scaled**3,
            np.sin(2.0 * np.pi * years),
            np.cos(2.0 * np.pi * years),
            np.sin(4.0 * np.pi * years),
            np.cos(4.0 * np.pi * years),
        ]
    )
    return np.pad(smooth, ((0, 0), (0, padded - count))).astype(np.float32)


def fit_operator(smooth, epochs, count):
    steps = epochs.shape[0]
    index = lax.broadcasted_iota(jnp.int32, (steps, smooth.shape[1]), 1)
    which = lax.broadcasted_iota(jnp.int32, (steps, smooth.shape[1]), 0)
    start = jnp.zeros_like(index)
    for e in range(steps):
        start = jnp.where(which == e, epochs[e], start)
    jumps = jnp.where((index >= start) & (index < count), 1.0, 0.0)
    right = jnp.concatenate([smooth, jumps], axis=0)
    terms = right.shape[0]
    normal = lax.dot_general(
        right,
        right,
        (((1,), (1,)), ((), ())),
        precision=lax.Precision.HIGHEST,
        preferred_element_type=jnp.float32,
    )
    line = lax.broadcasted_iota(jnp.int32, (terms, terms), 0)
    left = normal + jnp.where(
        line == lax.broadcasted_iota(jnp.int32, (terms, terms), 1), RIDGE, 0.0
    )
    wide = lax.broadcasted_iota(jnp.int32, right.shape, 0)
    for j in range(terms):
        pivot = left[j : j + 1, j : j + 1]
        left_row = left[j : j + 1, :] / pivot
        right_row = right[j : j + 1, :] / pivot
        factor = left[:, j : j + 1]
        left = jnp.where(line == j, left_row, left - factor * left_row)
        right = jnp.where(wide == j, right_row, right - factor * right_row)
    return right


def incidence_matrix(pairs, count):
    dates = jnp.arange(count, dtype=jnp.int32)
    later = (pairs[:, 1:2] == dates[None, :]).astype(jnp.float32)
    earlier = (pairs[:, 0:1] == dates[None, :]).astype(jnp.float32)
    return later - earlier


MESH = pl.DeviceIdType.MESH
LANES = 128


def reference_counts(region, tile, rows, width):
    blocks = width // LANES
    line = lax.shift_right_arithmetic(region, width.bit_length() - 1) - tile * rows
    col = lax.bitwise_and(region, width - 1)
    block = lax.shift_right_arithmetic(col, LANES.bit_length() - 1)
    lane = lax.bitwise_and(col, LANES - 1)
    key = jnp.where((line >= 0) & (line < rows), block * rows + line, -1)
    listed = region.shape[1]
    spots = lax.broadcasted_iota(jnp.int32, (blocks * rows, listed), 0) == key
    lanes = lax.broadcasted_iota(jnp.int32, (LANES, listed), 0) == lane
    return lax.dot_general(
        jnp.where(spots, 1.0, 0.0),
        jnp.where(lanes, 1.0, 0.0),
        (((1,), (1,)), ((), ())),
        preferred_element_type=jnp.float32,
    )


def exchange(
    dims, epochs, ifgs, inverse, region, smooth,
    moved, gathered, fit,
    sent, piece, counts, local, sums, sem,
):
    nx, nz, nc, tiles = dims
    group = nx * nz * nc
    half = nz // 2
    tile = lax.axis_index("tile")
    me = lax.axis_index("ifg")
    my_c = lax.rem(me, nc)
    my_z = lax.rem(lax.div(me, nc), nz)
    my_x = lax.div(me, nc * nz)

    def place(step):
        plane = lax.div(step, nx * nc)
        inner = lax.rem(step, nx * nc)
        j = lax.div(plane + 1, 2)
        odd = lax.rem(plane, 2)
        dz = odd * (half - j) + (1 - odd) * (half + j)
        dx = nx - 1 - lax.div(inner, nc)
        dc = nc - 1 - lax.rem(inner, nc)
        return lax.rem(my_x + dx, nx), lax.rem(my_z + dz, nz), lax.rem(my_c + dc, nc)

    def device(x, z, c):
        return {"ifg": (x * nz + z) * nc + c, "tile": tile}

    barrier = pltpu.get_barrier_semaphore()

    def greet(step, carry):
        pl.semaphore_signal(
            barrier, inc=1, device_id=device(*place(step)), device_id_type=MESH
        )
        return carry

    lax.fori_loop(0, group - 1, greet, 0)
    for d in range(1, tiles):
        pl.semaphore_signal(
            barrier,
            inc=1,
            device_id={"ifg": me, "tile": lax.rem(tile + d, tiles)},
            device_id_type=MESH,
        )

    count, rows, width = ifgs.shape
    dates = inverse.shape[1]
    piece[...] = jnp.zeros_like(piece)
    last = -(-dates // LANES) - 1
    for q in range(last + 1):
        lo, hi = q * LANES, min(q * LANES + LANES, dates)

        @pl.when(tile == q if q < last else tile >= last)
        def _(lo=lo, hi=hi):
            for k in range(count):
                piece[k // 2, k % 2 : k % 2 + 1, : hi - lo] = inverse[k : k + 1, lo:hi]

    own = pltpu.make_async_copy(piece, gathered.at[my_c, tile, my_x, my_z], sem.at[0])
    own.start()

    counts[...] = reference_counts(region[...], tile, rows, width)

    def collect(block, total):
        col = pl.multiple_of(block * LANES, LANES)
        values = ifgs[:, :, pl.ds(col, LANES)].astype(jnp.float32)
        return total + values * counts[pl.ds(block * rows, rows), :][None]

    local[...] = lax.fori_loop(
        0, width // LANES, collect, jnp.zeros((count, rows, LANES), jnp.float32)
    )
    pl.semaphore_wait(barrier, group - 1 + tiles - 1)

    def partial_copy(d):
        return pltpu.make_async_remote_copy(
            src_ref=local,
            dst_ref=sums.at[d - 1],
            send_sem=sem.at[d],
            recv_sem=sem.at[tiles + d],
            device_id={"ifg": me, "tile": lax.rem(tile + d, tiles)},
            device_id_type=MESH,
        )

    for d in range(1, tiles):
        partial_copy(d).start()

    base = 2 * tiles

    def z_copy(dz, ref):
        return pltpu.make_async_remote_copy(
            src_ref=ref,
            dst_ref=gathered.at[my_c, tile, my_x, my_z],
            send_sem=sem.at[base],
            recv_sem=sem.at[base + 1],
            device_id=device(my_x, lax.rem(my_z + dz, nz), my_c),
            device_id_type=MESH,
        )

    def send_z(i, carry):
        j = lax.div(i + 1, 2)
        odd = lax.rem(i, 2)
        z_copy(odd * (half - j) + (1 - odd) * (half + j), piece).start()
        return carry

    lax.fori_loop(0, nz - 1, send_z, 0)
    fit[...] = fit_operator(smooth[...], epochs, dates)

    for d in range(1, tiles):
        partial_copy(d).wait()
    total = local[...]
    for d in range(1, tiles):
        total = total + sums[d - 1]
    mean = jnp.sum(total, axis=(1, 2), keepdims=True) / region.shape[1]
    mean = jnp.broadcast_to(mean, (count, rows, LANES))

    def corrected(x, z, c):
        col = ((x * nz + z) * nc + c) * LANES
        values = ifgs[:, :, pl.ds(pl.multiple_of(col, LANES), LANES)].astype(jnp.float32)
        return (values - mean).astype(jnp.bfloat16)

    def prepare(step, carry):
        sent[step] = corrected(*place(step))
        return carry

    def block_copy(step):
        return pltpu.make_async_remote_copy(
            src_ref=sent.at[step],
            dst_ref=moved.at[my_c, my_x, my_z],
            send_sem=sem.at[base + 2],
            recv_sem=sem.at[base + 3],
            device_id=device(*place(step)),
            device_id_type=MESH,
        )

    def send_block(step, carry):
        block_copy(step).start()
        return carry

    plane = nx * nc
    first = plane * 5
    lax.fori_loop(0, plane, prepare, 0)

    def both(step, carry):
        send_block(step, carry)
        return prepare(step + plane, carry)

    lax.fori_loop(0, first, both, 0)

    own.wait()
    arrived = pltpu.make_async_remote_copy(
        src_ref=gathered.at[0, 0, 0, pl.ds(0, nz - 1)],
        dst_ref=gathered.at[0, 0, 0, pl.ds(0, nz - 1)],
        send_sem=sem.at[base],
        recv_sem=sem.at[base + 1],
        device_id=device(my_x, lax.rem(my_z + 1, nz), my_c),
        device_id_type=MESH,
    )
    arrived.wait()

    def x_copy(d):
        return pltpu.make_async_remote_copy(
            src_ref=gathered.at[my_c, tile, my_x],
            dst_ref=gathered.at[my_c, tile, my_x],
            send_sem=sem.at[base + 2 + 2 * d],
            recv_sem=sem.at[base + 3 + 2 * d],
            device_id=device(lax.rem(my_x + d, nx), my_z, my_c),
            device_id_type=MESH,
        )

    for d in range(1, nx):
        x_copy(d).start()

    lax.fori_loop(first, group - 1 - plane, both, 0)
    lax.fori_loop(group - 1 - plane, group - 1, send_block, 0)
    moved[my_c, my_x, my_z] = corrected(my_x, my_z, my_c)

    for d in range(1, nx):
        x_copy(d).wait()

    over = base + 2 + 2 * nx

    def tile_copy(d):
        return pltpu.make_async_remote_copy(
            src_ref=gathered.at[my_c, tile],
            dst_ref=gathered.at[my_c, tile],
            send_sem=sem.at[over + 2 * d],
            recv_sem=sem.at[over + 1 + 2 * d],
            device_id={"ifg": me, "tile": lax.rem(tile + d, tiles)},
            device_id_type=MESH,
        )

    for d in range(1, tiles):
        tile_copy(d).start()
    for d in range(1, tiles):
        tile_copy(d).wait()
    core = pltpu.make_async_remote_copy(
        src_ref=gathered.at[my_c],
        dst_ref=gathered.at[my_c],
        send_sem=sem.at[over],
        recv_sem=sem.at[over + 1],
        device_id=device(my_x, my_z, lax.rem(my_c + 1, nc)),
        device_id_type=MESH,
    )
    core.start()
    everything = pltpu.make_async_remote_copy(
        src_ref=sent.at[pl.ds(0, group - 1)],
        dst_ref=sent.at[pl.ds(0, group - 1)],
        send_sem=sem.at[base + 2],
        recv_sem=sem.at[base + 3],
        device_id=device(my_x, lax.rem(my_z + 1, nz), my_c),
        device_id_type=MESH,
    )
    everything.wait()
    core.wait()


def shards(ifgs, pairs, pseudo_inverse, ref_pixels, epochs, physical):
    nx, nz, nc = physical
    count, row_count, col_total = ifgs.shape
    group = lax.axis_size("ifg")
    tiles = lax.axis_size("tile")
    date_count = pseudo_inverse.shape[0]
    padded = -(-date_count // LANES) * LANES
    pairs_up = -(-count // 2)
    vmem = pl.BlockSpec(memory_space=pltpu.VMEM)
    smooth = jnp.asarray(smooth_columns(date_count, padded))
    terms = smooth.shape[0] + epochs.shape[0]
    moved, gathered, fit = pl.pallas_call(
        functools.partial(exchange, (nx, nz, nc, tiles)),
        out_shape=(
            jax.ShapeDtypeStruct((nc, nx, nz, count, row_count, LANES), jnp.bfloat16),
            jax.ShapeDtypeStruct((nc, tiles, nx, nz, pairs_up, 2, LANES), jnp.bfloat16),
            jax.ShapeDtypeStruct((terms, padded), jnp.float32),
        ),
        in_specs=[pl.BlockSpec(memory_space=pltpu.SMEM)] + [vmem] * 4,
        out_specs=(vmem,) * 3,
        scratch_shapes=[
            pltpu.VMEM((group, count, row_count, LANES), jnp.bfloat16),
            pltpu.VMEM((pairs_up, 2, LANES), jnp.bfloat16),
            pltpu.VMEM((col_total // LANES * row_count, LANES), jnp.float32),
            pltpu.VMEM((count, row_count, LANES), jnp.float32),
            pltpu.VMEM((tiles - 1, count, row_count, LANES), jnp.float32),
            pltpu.SemaphoreType.DMA((4 * tiles + 2 * nx + 4,)),
        ],
        compiler_params=pltpu.CompilerParams(collective_id=0, has_side_effects=True),
    )(epochs, ifgs, pseudo_inverse.T, ref_pixels[None, :], smooth)
    total = group * count
    pixel_rows = moved.reshape(total, row_count * LANES)
    operator = gathered[:, : padded // LANES].transpose(0, 2, 3, 4, 5, 1, 6)
    operator = operator.reshape(group, 2 * pairs_up, padded)[:, :count, :date_count]
    displacement = lax.dot_general(
        operator.reshape(total, date_count),
        pixel_rows,
        (((0,), (0,)), ((), ())),
        preferred_element_type=jnp.float32,
    )
    fit = fit[:, :date_count]
    coeffs = jnp.dot(
        fit, displacement, precision=lax.Precision.HIGHEST, preferred_element_type=jnp.float32
    )
    ordered = pairs.reshape(nx, nz, nc, count, 2).transpose(2, 0, 1, 3, 4).reshape(total, 2)
    incidence = incidence_matrix(ordered, date_count)
    predicted = jnp.dot(
        incidence, displacement, precision=lax.Precision.HIGHEST, preferred_element_type=jnp.float32
    )
    misfit = pixel_rows.astype(jnp.float32) - predicted
    spread = jnp.sqrt(jnp.mean(misfit * misfit, axis=0) + EPS)
    return (
        coeffs.reshape(terms, row_count, LANES),
        spread.reshape(row_count, LANES),
    )


def solution(mesh):
    nx, nc = 4, 2
    nz = mesh.shape["ifg"] // (nx * nc)
    in_specs = (P("ifg", "tile", None), P(), P(None, "ifg"), P(), P())
    out_specs = (P(None, "tile", "ifg"), P("tile", "ifg"))
    run = functools.partial(shards, physical=(nx, nz, nc))
    return jax.shard_map(run, mesh=mesh, in_specs=in_specs, out_specs=out_specs, check_vma=False)
```

```python
import functools

import jax
import jax.numpy as jnp
import numpy as np
from jax import lax
from jax.experimental import pallas as pl
from jax.experimental.pallas import tpu as pltpu
from jax.sharding import PartitionSpec as P

EPS = 1e-06
RIDGE = 1.0


def smooth_columns(count, padded):
    days = np.arange(count, dtype=np.float64)
    scaled = 2.0 * days / (count - 1) - 1.0
    years = days * 12.0 / 365.25
    smooth = np.stack(
        [
            np.ones_like(days),
            scaled,
            scaled**2,
            scaled**3,
            np.sin(2.0 * np.pi * years),
            np.cos(2.0 * np.pi * years),
            np.sin(4.0 * np.pi * years),
            np.cos(4.0 * np.pi * years),
        ]
    )
    return np.pad(smooth, ((0, 0), (0, padded - count))).astype(np.float32)


def fit_operator(smooth, epochs, count):
    steps = epochs.shape[0]
    index = lax.broadcasted_iota(jnp.int32, (steps, smooth.shape[1]), 1)
    which = lax.broadcasted_iota(jnp.int32, (steps, smooth.shape[1]), 0)
    start = jnp.zeros_like(index)
    for e in range(steps):
        start = jnp.where(which == e, epochs[e], start)
    jumps = jnp.where((index >= start) & (index < count), 1.0, 0.0)
    right = jnp.concatenate([smooth, jumps], axis=0)
    terms = right.shape[0]
    normal = lax.dot_general(
        right,
        right,
        (((1,), (1,)), ((), ())),
        precision=lax.Precision.HIGHEST,
        preferred_element_type=jnp.float32,
    )
    line = lax.broadcasted_iota(jnp.int32, (terms, terms), 0)
    left = normal + jnp.where(
        line == lax.broadcasted_iota(jnp.int32, (terms, terms), 1), RIDGE, 0.0
    )
    wide = lax.broadcasted_iota(jnp.int32, right.shape, 0)
    for j in range(terms):
        pivot = left[j : j + 1, j : j + 1]
        left_row = left[j : j + 1, :] / pivot
        right_row = right[j : j + 1, :] / pivot
        factor = left[:, j : j + 1]
        left = jnp.where(line == j, left_row, left - factor * left_row)
        right = jnp.where(wide == j, right_row, right - factor * right_row)
    return right


def incidence_matrix(pairs, count):
    dates = jnp.arange(count, dtype=jnp.int32)
    later = (pairs[:, 1:2] == dates[None, :]).astype(jnp.float32)
    earlier = (pairs[:, 0:1] == dates[None, :]).astype(jnp.float32)
    return later - earlier


MESH = pl.DeviceIdType.MESH
LANES = 128


def reference_counts(region, tile, rows, width):
    blocks = width // LANES
    line = lax.shift_right_arithmetic(region, width.bit_length() - 1) - tile * rows
    col = lax.bitwise_and(region, width - 1)
    block = lax.shift_right_arithmetic(col, LANES.bit_length() - 1)
    lane = lax.bitwise_and(col, LANES - 1)
    key = jnp.where((line >= 0) & (line < rows), block * rows + line, -1)
    listed = region.shape[1]
    spots = lax.broadcasted_iota(jnp.int32, (blocks * rows, listed), 0) == key
    lanes = lax.broadcasted_iota(jnp.int32, (LANES, listed), 0) == lane
    return lax.dot_general(
        jnp.where(spots, 1.0, 0.0),
        jnp.where(lanes, 1.0, 0.0),
        (((1,), (1,)), ((), ())),
        preferred_element_type=jnp.float32,
    )


def exchange(
    dims, epochs, ifgs, inverse, region, smooth,
    moved, gathered, fit,
    sent, piece, column, counts, local, sums, sem,
):
    nx, nz, nc, tiles = dims
    group = nx * nz * nc
    half = nz // 2
    tile = lax.axis_index("tile")
    me = lax.axis_index("ifg")
    my_c = lax.rem(me, nc)
    my_z = lax.rem(lax.div(me, nc), nz)
    my_x = lax.div(me, nc * nz)

    def place(step):
        plane = lax.div(step, nx * nc)
        inner = lax.rem(step, nx * nc)
        j = lax.div(plane + 1, 2)
        odd = lax.rem(plane, 2)
        dz = odd * (half - j) + (1 - odd) * (half + j)
        dx = nx - 1 - lax.div(inner, nc)
        dc = nc - 1 - lax.rem(inner, nc)
        return lax.rem(my_x + dx, nx), lax.rem(my_z + dz, nz), lax.rem(my_c + dc, nc)

    def device(x, z, c):
        return {"ifg": (x * nz + z) * nc + c, "tile": tile}

    column[...] = jnp.zeros_like(column)
    barrier = pltpu.get_barrier_semaphore()

    def greet(step, carry):
        pl.semaphore_signal(
            barrier, inc=1, device_id=device(*place(step)), device_id_type=MESH
        )
        return carry

    lax.fori_loop(0, group - 1, greet, 0)
    for d in range(1, tiles):
        pl.semaphore_signal(
            barrier,
            inc=1,
            device_id={"ifg": me, "tile": lax.rem(tile + d, tiles)},
            device_id_type=MESH,
        )

    count, rows, width = ifgs.shape
    dates = inverse.shape[1]
    piece[...] = jnp.zeros_like(piece)
    last = -(-dates // LANES) - 1
    for q in range(last + 1):
        lo, hi = q * LANES, min(q * LANES + LANES, dates)

        @pl.when(tile == q if q < last else tile >= last)
        def _(lo=lo, hi=hi):
            piece[:count, : hi - lo] = inverse[:, lo:hi]

    column[my_z] = piece[...]

    counts[...] = reference_counts(region[...], tile, rows, width)

    def collect(block, total):
        col = pl.multiple_of(block * LANES, LANES)
        values = ifgs[:, :, pl.ds(col, LANES)].astype(jnp.float32)
        return total + values * counts[pl.ds(block * rows, rows), :][None]

    local[...] = lax.fori_loop(
        0, width // LANES, collect, jnp.zeros((count, rows, LANES), jnp.float32)
    )
    pl.semaphore_wait(barrier, group - 1 + tiles - 1)

    def partial_copy(d):
        return pltpu.make_async_remote_copy(
            src_ref=local,
            dst_ref=sums.at[d - 1],
            send_sem=sem.at[d],
            recv_sem=sem.at[tiles + d],
            device_id={"ifg": me, "tile": lax.rem(tile + d, tiles)},
            device_id_type=MESH,
        )

    for d in range(1, tiles):
        partial_copy(d).start()

    base = 2 * tiles
    even = -(-count // 2) * 2

    def z_copy(dz, ref):
        return pltpu.make_async_remote_copy(
            src_ref=ref,
            dst_ref=column.at[my_z, pl.ds(0, even)],
            send_sem=sem.at[base],
            recv_sem=sem.at[base + 1],
            device_id=device(my_x, lax.rem(my_z + dz, nz), my_c),
            device_id_type=MESH,
        )

    def send_z(i, carry):
        j = lax.div(i + 1, 2)
        odd = lax.rem(i, 2)
        z_copy(odd * (half - j) + (1 - odd) * (half + j), piece.at[pl.ds(0, even)]).start()
        return carry

    lax.fori_loop(0, nz - 1, send_z, 0)
    fit[...] = fit_operator(smooth[...], epochs, dates)

    for d in range(1, tiles):
        partial_copy(d).wait()
    total = local[...]
    for d in range(1, tiles):
        total = total + sums[d - 1]
    mean = jnp.sum(total, axis=(1, 2), keepdims=True) / region.shape[1]
    mean = jnp.broadcast_to(mean, (count, rows, LANES))

    def corrected(x, z, c):
        col = ((x * nz + z) * nc + c) * LANES
        values = ifgs[:, :, pl.ds(pl.multiple_of(col, LANES), LANES)].astype(jnp.float32)
        return (values - mean).astype(jnp.bfloat16)

    def prepare(step, carry):
        sent[step] = corrected(*place(step))
        return carry

    def block_copy(step):
        return pltpu.make_async_remote_copy(
            src_ref=sent.at[step],
            dst_ref=moved.at[my_c, my_x, my_z],
            send_sem=sem.at[base + 2],
            recv_sem=sem.at[base + 3],
            device_id=device(*place(step)),
            device_id_type=MESH,
        )

    def send_block(step, carry):
        block_copy(step).start()
        return carry

    plane = nx * nc
    first = plane * 5
    lax.fori_loop(0, plane, prepare, 0)

    def both(step, carry):
        send_block(step, carry)
        return prepare(step + plane, carry)

    lax.fori_loop(0, first, both, 0)

    arrived = pltpu.make_async_remote_copy(
        src_ref=column.at[pl.ds(0, nz - 1), pl.ds(0, even)],
        dst_ref=column.at[pl.ds(0, nz - 1), pl.ds(0, even)],
        send_sem=sem.at[base],
        recv_sem=sem.at[base + 1],
        device_id=device(my_x, lax.rem(my_z + 1, nz), my_c),
        device_id_type=MESH,
    )
    arrived.wait()
    tall = column.shape[1]
    target = lax.broadcasted_iota(jnp.int32, (nz * count, nz * tall), 0)
    source = lax.broadcasted_iota(jnp.int32, (nz * count, nz * tall), 1)
    line = lax.bitwise_and(source, tall - 1)
    block = lax.shift_right_arithmetic(source, tall.bit_length() - 1)
    pick = jnp.where((line < count) & (block * count + line == target), 1.0, 0.0)
    gathered[my_c, tile, my_x] = jnp.dot(
        pick.astype(jnp.bfloat16),
        column[...].reshape(nz * tall, LANES),
        preferred_element_type=jnp.float32,
    ).astype(jnp.bfloat16)
    second = first + 2 * plane
    lax.fori_loop(first, second, both, 0)

    def x_copy(d):
        return pltpu.make_async_remote_copy(
            src_ref=gathered.at[my_c, tile, my_x],
            dst_ref=gathered.at[my_c, tile, my_x],
            send_sem=sem.at[base + 2 + 2 * d],
            recv_sem=sem.at[base + 3 + 2 * d],
            device_id=device(lax.rem(my_x + d, nx), my_z, my_c),
            device_id_type=MESH,
        )

    for d in range(1, nx):
        x_copy(d).start()

    lax.fori_loop(second, group - 1 - plane, both, 0)
    lax.fori_loop(group - 1 - plane, group - 1, send_block, 0)
    moved[my_c, my_x, my_z] = corrected(my_x, my_z, my_c)

    for d in range(1, nx):
        x_copy(d).wait()

    over = base + 2 + 2 * nx

    def tile_copy(d):
        return pltpu.make_async_remote_copy(
            src_ref=gathered.at[my_c, tile],
            dst_ref=gathered.at[my_c, tile],
            send_sem=sem.at[over + 2 * d],
            recv_sem=sem.at[over + 1 + 2 * d],
            device_id={"ifg": me, "tile": lax.rem(tile + d, tiles)},
            device_id_type=MESH,
        )

    for d in range(1, tiles):
        tile_copy(d).start()
    for d in range(1, tiles):
        tile_copy(d).wait()
    core = pltpu.make_async_remote_copy(
        src_ref=gathered.at[my_c],
        dst_ref=gathered.at[my_c],
        send_sem=sem.at[over],
        recv_sem=sem.at[over + 1],
        device_id=device(my_x, my_z, lax.rem(my_c + 1, nc)),
        device_id_type=MESH,
    )
    core.start()
    everything = pltpu.make_async_remote_copy(
        src_ref=sent.at[pl.ds(0, group - 1)],
        dst_ref=sent.at[pl.ds(0, group - 1)],
        send_sem=sem.at[base + 2],
        recv_sem=sem.at[base + 3],
        device_id=device(my_x, lax.rem(my_z + 1, nz), my_c),
        device_id_type=MESH,
    )
    everything.wait()
    core.wait()


def shards(ifgs, pairs, pseudo_inverse, ref_pixels, epochs, physical):
    nx, nz, nc = physical
    count, row_count, col_total = ifgs.shape
    group = lax.axis_size("ifg")
    tiles = lax.axis_size("tile")
    date_count = pseudo_inverse.shape[0]
    padded = -(-date_count // LANES) * LANES
    tall = 16
    vmem = pl.BlockSpec(memory_space=pltpu.VMEM)
    smooth = jnp.asarray(smooth_columns(date_count, padded))
    terms = smooth.shape[0] + epochs.shape[0]
    moved, gathered, fit = pl.pallas_call(
        functools.partial(exchange, (nx, nz, nc, tiles)),
        out_shape=(
            jax.ShapeDtypeStruct((nc, nx, nz, count, row_count, LANES), jnp.bfloat16),
            jax.ShapeDtypeStruct((nc, tiles, nx, nz * count, LANES), jnp.bfloat16),
            jax.ShapeDtypeStruct((terms, padded), jnp.float32),
        ),
        in_specs=[pl.BlockSpec(memory_space=pltpu.SMEM)] + [vmem] * 4,
        out_specs=(vmem,) * 3,
        scratch_shapes=[
            pltpu.VMEM((group, count, row_count, LANES), jnp.bfloat16),
            pltpu.VMEM((tall, LANES), jnp.bfloat16),
            pltpu.VMEM((nz, tall, LANES), jnp.bfloat16),
            pltpu.VMEM((col_total // LANES * row_count, LANES), jnp.float32),
            pltpu.VMEM((count, row_count, LANES), jnp.float32),
            pltpu.VMEM((tiles - 1, count, row_count, LANES), jnp.float32),
            pltpu.SemaphoreType.DMA((4 * tiles + 2 * nx + 4,)),
        ],
        compiler_params=pltpu.CompilerParams(collective_id=0, has_side_effects=True),
    )(epochs, ifgs, pseudo_inverse.T, ref_pixels[None, :], smooth)
    total = group * count
    pixel_rows = moved.reshape(total, row_count * LANES)
    operator = gathered[:, : padded // LANES].transpose(0, 2, 3, 1, 4).reshape(total, padded)
    displacement = lax.dot_general(
        operator,
        pixel_rows,
        (((0,), (0,)), ((), ())),
        preferred_element_type=jnp.float32,
    )
    coeffs = jnp.dot(
        fit, displacement, precision=lax.Precision.HIGHEST, preferred_element_type=jnp.float32
    )
    ordered = pairs.reshape(nx, nz, nc, count, 2).transpose(2, 0, 1, 3, 4).reshape(total, 2)
    incidence = incidence_matrix(ordered, padded)
    predicted = jnp.dot(
        incidence, displacement, precision=lax.Precision.HIGH, preferred_element_type=jnp.float32
    )
    misfit = pixel_rows.astype(jnp.float32) - predicted
    spread = jnp.sqrt(jnp.mean(misfit * misfit, axis=0) + EPS)
    return (
        coeffs.reshape(terms, row_count, LANES),
        spread.reshape(row_count, LANES),
    )


def solution(mesh):
    nx, nc = 4, 2
    nz = mesh.shape["ifg"] // (nx * nc)
    in_specs = (P("ifg", "tile", None), P(), P(None, "ifg"), P(), P())
    out_specs = (P(None, "tile", "ifg"), P("tile", "ifg"))
    run = functools.partial(shards, physical=(nx, nz, nc))
    return jax.shard_map(run, mesh=mesh, in_specs=in_specs, out_specs=out_specs, check_vma=False)
```

```python
import functools

import jax
import jax.numpy as jnp
import numpy as np
from jax import lax
from jax.experimental import pallas as pl
from jax.experimental.pallas import tpu as pltpu
from jax.sharding import PartitionSpec as P

EPS = 1e-06
RIDGE = 1.0


def smooth_columns(count, padded):
    days = np.arange(count, dtype=np.float64)
    scaled = 2.0 * days / (count - 1) - 1.0
    years = days * 12.0 / 365.25
    smooth = np.stack(
        [
            np.ones_like(days),
            scaled,
            scaled**2,
            scaled**3,
            np.sin(2.0 * np.pi * years),
            np.cos(2.0 * np.pi * years),
            np.sin(4.0 * np.pi * years),
            np.cos(4.0 * np.pi * years),
        ]
    )
    return np.pad(smooth, ((0, 0), (0, padded - count))).astype(np.float32)


def fit_operator(smooth, epochs, count):
    steps = epochs.shape[0]
    index = lax.broadcasted_iota(jnp.int32, (steps, smooth.shape[1]), 1)
    which = lax.broadcasted_iota(jnp.int32, (steps, smooth.shape[1]), 0)
    start = jnp.zeros_like(index)
    for e in range(steps):
        start = jnp.where(which == e, epochs[e], start)
    jumps = jnp.where((index >= start) & (index < count), 1.0, 0.0)
    right = jnp.concatenate([smooth, jumps], axis=0)
    terms = right.shape[0]
    normal = lax.dot_general(
        right,
        right,
        (((1,), (1,)), ((), ())),
        precision=lax.Precision.HIGHEST,
        preferred_element_type=jnp.float32,
    )
    line = lax.broadcasted_iota(jnp.int32, (terms, terms), 0)
    left = normal + jnp.where(
        line == lax.broadcasted_iota(jnp.int32, (terms, terms), 1), RIDGE, 0.0
    )
    wide = lax.broadcasted_iota(jnp.int32, right.shape, 0)
    for j in range(terms):
        pivot = left[j : j + 1, j : j + 1]
        left_row = left[j : j + 1, :] / pivot
        right_row = right[j : j + 1, :] / pivot
        factor = left[:, j : j + 1]
        left = jnp.where(line == j, left_row, left - factor * left_row)
        right = jnp.where(wide == j, right_row, right - factor * right_row)
    return right


def incidence_matrix(pairs, count):
    dates = jnp.arange(count, dtype=jnp.int32)
    later = (pairs[:, 1:2] == dates[None, :]).astype(jnp.float32)
    earlier = (pairs[:, 0:1] == dates[None, :]).astype(jnp.float32)
    return later - earlier


MESH = pl.DeviceIdType.MESH
LANES = 128


def reference_counts(region, tile, rows, width):
    blocks = width // LANES
    line = lax.shift_right_arithmetic(region, width.bit_length() - 1) - tile * rows
    col = lax.bitwise_and(region, width - 1)
    block = lax.shift_right_arithmetic(col, LANES.bit_length() - 1)
    lane = lax.bitwise_and(col, LANES - 1)
    key = jnp.where((line >= 0) & (line < rows), block * rows + line, -1)
    listed = region.shape[1]
    spots = lax.broadcasted_iota(jnp.int32, (blocks * rows, listed), 0) == key
    lanes = lax.broadcasted_iota(jnp.int32, (LANES, listed), 0) == lane
    return lax.dot_general(
        jnp.where(spots, 1.0, 0.0),
        jnp.where(lanes, 1.0, 0.0),
        (((1,), (1,)), ((), ())),
        preferred_element_type=jnp.float32,
    )


def exchange(
    dims, epochs, ifgs, inverse, region, smooth,
    moved, gathered, fit,
    sent, relayed, piece, column, counts, local, sums, sem,
):
    nx, nz, nc, tiles = dims
    group = nx * nz * nc
    half = nz // 2
    tile = lax.axis_index("tile")
    me = lax.axis_index("ifg")
    my_c = lax.rem(me, nc)
    my_z = lax.rem(lax.div(me, nc), nz)
    my_x = lax.div(me, nc * nz)

    def place(step):
        plane = lax.div(step, nx * nc)
        inner = lax.rem(step, nx * nc)
        j = lax.div(plane + 1, 2)
        odd = lax.rem(plane, 2)
        dz = odd * (half - j) + (1 - odd) * (half + j)
        dx = nx - 1 - lax.div(inner, nc)
        dc = nc - 1 - lax.rem(inner, nc)
        return lax.rem(my_x + dx, nx), lax.rem(my_z + dz, nz), lax.rem(my_c + dc, nc)

    def device(x, z, c):
        return {"ifg": (x * nz + z) * nc + c, "tile": tile}

    column[...] = jnp.zeros_like(column)
    barrier = pltpu.get_barrier_semaphore()

    def greet(step, carry):
        pl.semaphore_signal(
            barrier, inc=1, device_id=device(*place(step)), device_id_type=MESH
        )
        return carry

    lax.fori_loop(0, group - 1, greet, 0)
    for d in range(1, tiles):
        pl.semaphore_signal(
            barrier,
            inc=1,
            device_id={"ifg": me, "tile": lax.rem(tile + d, tiles)},
            device_id_type=MESH,
        )

    count, rows, width = ifgs.shape
    dates = inverse.shape[1]
    piece[...] = jnp.zeros_like(piece)
    last = -(-dates // LANES) - 1
    for q in range(last + 1):
        lo, hi = q * LANES, min(q * LANES + LANES, dates)

        @pl.when(tile == q if q < last else tile >= last)
        def _(lo=lo, hi=hi):
            piece[:count, : hi - lo] = inverse[:, lo:hi]

    column[my_z] = piece[...]

    counts[...] = reference_counts(region[...], tile, rows, width)

    def collect(block, total):
        col = pl.multiple_of(block * LANES, LANES)
        values = ifgs[:, :, pl.ds(col, LANES)].astype(jnp.float32)
        return total + values * counts[pl.ds(block * rows, rows), :][None]

    local[...] = lax.fori_loop(
        0, width // LANES, collect, jnp.zeros((count, rows, LANES), jnp.float32)
    )
    pl.semaphore_wait(barrier, group - 1 + tiles - 1)

    def partial_copy(d):
        return pltpu.make_async_remote_copy(
            src_ref=local,
            dst_ref=sums.at[d - 1],
            send_sem=sem.at[d],
            recv_sem=sem.at[tiles + d],
            device_id={"ifg": me, "tile": lax.rem(tile + d, tiles)},
            device_id_type=MESH,
        )

    for d in range(1, tiles):
        partial_copy(d).start()

    base = 2 * tiles
    even = -(-count // 2) * 2

    def z_copy(dz, ref):
        return pltpu.make_async_remote_copy(
            src_ref=ref,
            dst_ref=column.at[my_z, pl.ds(0, even)],
            send_sem=sem.at[base],
            recv_sem=sem.at[base + 1],
            device_id=device(my_x, lax.rem(my_z + dz, nz), my_c),
            device_id_type=MESH,
        )

    def send_z(i, carry):
        j = lax.div(i + 1, 2)
        odd = lax.rem(i, 2)
        z_copy(odd * (half - j) + (1 - odd) * (half + j), piece.at[pl.ds(0, even)]).start()
        return carry

    lax.fori_loop(0, nz - 1, send_z, 0)

    for d in range(1, tiles):
        partial_copy(d).wait()
    total = local[...]
    for d in range(1, tiles):
        total = total + sums[d - 1]
    mean = jnp.sum(total, axis=(1, 2), keepdims=True) / region.shape[1]
    mean = jnp.broadcast_to(mean, (count, rows, LANES))

    def corrected(x, z, c):
        col = ((x * nz + z) * nc + c) * LANES
        values = ifgs[:, :, pl.ds(pl.multiple_of(col, LANES), LANES)].astype(jnp.float32)
        return (values - mean).astype(jnp.bfloat16)

    def prepare(step, carry):
        sent[step] = corrected(*place(step))
        return carry

    def block_copy(step):
        return pltpu.make_async_remote_copy(
            src_ref=sent.at[step],
            dst_ref=moved.at[my_c, my_x, my_z],
            send_sem=sem.at[base + 2],
            recv_sem=sem.at[base + 3],
            device_id=device(*place(step)),
            device_id_type=MESH,
        )

    def send_block(step, carry):
        block_copy(step).start()
        return carry

    plane = nx * nc
    first = plane * 5
    hops = plane // 2
    last_sem = sem.shape[0] - 2

    def relay_copy(slot, ref):
        return pltpu.make_async_remote_copy(
            src_ref=ref,
            dst_ref=slot,
            send_sem=sem.at[last_sem],
            recv_sem=sem.at[last_sem + 1],
            device_id=device(my_x, lax.rem(my_z + nz - 1, nz), my_c),
            device_id_type=MESH,
        )

    def pass_on(step, carry):
        x, z, c = place(step)
        pltpu.make_async_remote_copy(
            src_ref=relayed.at[step],
            dst_ref=moved.at[my_c, my_x, lax.rem(my_z + 1, nz)],
            send_sem=sem.at[base + 2],
            recv_sem=sem.at[base + 3],
            device_id=device(x, lax.rem(z + 1, nz), c),
            device_id_type=MESH,
        ).start()
        return carry

    lax.fori_loop(0, plane, prepare, 0)

    def both(step, carry):
        send_block(step, carry)
        return prepare(step + plane, carry)

    def both_relayed(step, carry):
        relay_copy(relayed.at[step], sent.at[step]).start()
        return prepare(step + plane, carry)

    lax.fori_loop(0, hops, both_relayed, 0)
    lax.fori_loop(hops, 3 * plane, both, 0)
    relay_copy(relayed, relayed).wait()
    lax.fori_loop(0, hops, pass_on, 0)
    lax.fori_loop(3 * plane, first, both, 0)

    arrived = pltpu.make_async_remote_copy(
        src_ref=column.at[pl.ds(0, nz - 1), pl.ds(0, even)],
        dst_ref=column.at[pl.ds(0, nz - 1), pl.ds(0, even)],
        send_sem=sem.at[base],
        recv_sem=sem.at[base + 1],
        device_id=device(my_x, lax.rem(my_z + 1, nz), my_c),
        device_id_type=MESH,
    )
    arrived.wait()
    tall = column.shape[1]
    target = lax.broadcasted_iota(jnp.int32, (nz * count, nz * tall), 0)
    source = lax.broadcasted_iota(jnp.int32, (nz * count, nz * tall), 1)
    line = lax.bitwise_and(source, tall - 1)
    block = lax.shift_right_arithmetic(source, tall.bit_length() - 1)
    pick = jnp.where((line < count) & (block * count + line == target), 1.0, 0.0)
    gathered[my_c, tile, my_x] = jnp.dot(
        pick.astype(jnp.bfloat16),
        column[...].reshape(nz * tall, LANES),
        preferred_element_type=jnp.float32,
    ).astype(jnp.bfloat16)
    second = first + 2 * plane
    lax.fori_loop(first, second, both, 0)

    def x_copy(d):
        return pltpu.make_async_remote_copy(
            src_ref=gathered.at[my_c, tile, my_x],
            dst_ref=gathered.at[my_c, tile, my_x],
            send_sem=sem.at[base + 2 + 2 * d],
            recv_sem=sem.at[base + 3 + 2 * d],
            device_id=device(lax.rem(my_x + d, nx), my_z, my_c),
            device_id_type=MESH,
        )

    for d in range(1, nx):
        x_copy(d).start()

    lax.fori_loop(second, group - 1 - plane, both, 0)
    lax.fori_loop(group - 1 - plane, group - 1, send_block, 0)
    fit[...] = fit_operator(smooth[...], epochs, dates)
    moved[my_c, my_x, my_z] = corrected(my_x, my_z, my_c)

    for d in range(1, nx):
        x_copy(d).wait()

    over = base + 2 + 2 * nx

    def tile_copy(d):
        return pltpu.make_async_remote_copy(
            src_ref=gathered.at[my_c, tile],
            dst_ref=gathered.at[my_c, tile],
            send_sem=sem.at[over + 2 * d],
            recv_sem=sem.at[over + 1 + 2 * d],
            device_id={"ifg": me, "tile": lax.rem(tile + d, tiles)},
            device_id_type=MESH,
        )

    for d in range(1, tiles):
        tile_copy(d).start()
    for d in range(1, tiles):
        tile_copy(d).wait()
    core = pltpu.make_async_remote_copy(
        src_ref=gathered.at[my_c],
        dst_ref=gathered.at[my_c],
        send_sem=sem.at[over],
        recv_sem=sem.at[over + 1],
        device_id=device(my_x, my_z, lax.rem(my_c + 1, nc)),
        device_id_type=MESH,
    )
    core.start()
    everything = pltpu.make_async_remote_copy(
        src_ref=sent.at[pl.ds(0, group - 1)],
        dst_ref=sent.at[pl.ds(0, group - 1)],
        send_sem=sem.at[base + 2],
        recv_sem=sem.at[base + 3],
        device_id=device(my_x, lax.rem(my_z + 1, nz), my_c),
        device_id_type=MESH,
    )
    everything.wait()
    core.wait()


def shards(ifgs, pairs, pseudo_inverse, ref_pixels, epochs, physical):
    nx, nz, nc = physical
    count, row_count, col_total = ifgs.shape
    group = lax.axis_size("ifg")
    tiles = lax.axis_size("tile")
    date_count = pseudo_inverse.shape[0]
    padded = -(-date_count // LANES) * LANES
    tall = 16
    vmem = pl.BlockSpec(memory_space=pltpu.VMEM)
    smooth = jnp.asarray(smooth_columns(date_count, padded))
    terms = smooth.shape[0] + epochs.shape[0]
    moved, gathered, fit = pl.pallas_call(
        functools.partial(exchange, (nx, nz, nc, tiles)),
        out_shape=(
            jax.ShapeDtypeStruct((nc, nx, nz, count, row_count, LANES), jnp.bfloat16),
            jax.ShapeDtypeStruct((nc, tiles, nx, nz * count, LANES), jnp.bfloat16),
            jax.ShapeDtypeStruct((terms, padded), jnp.float32),
        ),
        in_specs=[pl.BlockSpec(memory_space=pltpu.SMEM)] + [vmem] * 4,
        out_specs=(vmem,) * 3,
        scratch_shapes=[
            pltpu.VMEM((group, count, row_count, LANES), jnp.bfloat16),
            pltpu.VMEM((nx * nc // 2, count, row_count, LANES), jnp.bfloat16),
            pltpu.VMEM((tall, LANES), jnp.bfloat16),
            pltpu.VMEM((nz, tall, LANES), jnp.bfloat16),
            pltpu.VMEM((col_total // LANES * row_count, LANES), jnp.float32),
            pltpu.VMEM((count, row_count, LANES), jnp.float32),
            pltpu.VMEM((tiles - 1, count, row_count, LANES), jnp.float32),
            pltpu.SemaphoreType.DMA((4 * tiles + 2 * nx + 6,)),
        ],
        compiler_params=pltpu.CompilerParams(collective_id=0, has_side_effects=True),
    )(epochs, ifgs, pseudo_inverse.T, ref_pixels[None, :], smooth)
    total = group * count
    pixel_rows = moved.reshape(total, row_count * LANES)
    operator = gathered[:, : padded // LANES].transpose(0, 2, 3, 1, 4).reshape(total, padded)
    displacement = lax.dot_general(
        operator,
        pixel_rows,
        (((0,), (0,)), ((), ())),
        preferred_element_type=jnp.float32,
    )
    coeffs = jnp.dot(
        fit, displacement, precision=lax.Precision.HIGHEST, preferred_element_type=jnp.float32
    )
    ordered = pairs.reshape(nx, nz, nc, count, 2).transpose(2, 0, 1, 3, 4).reshape(total, 2)
    incidence = incidence_matrix(ordered, padded)
    predicted = jnp.dot(
        incidence, displacement, precision=lax.Precision.HIGH, preferred_element_type=jnp.float32
    )
    misfit = pixel_rows.astype(jnp.float32) - predicted
    spread = jnp.sqrt(jnp.mean(misfit * misfit, axis=0) + EPS)
    return (
        coeffs.reshape(terms, row_count, LANES),
        spread.reshape(row_count, LANES),
    )


def solution(mesh):
    nx, nc = 4, 2
    nz = mesh.shape["ifg"] // (nx * nc)
    in_specs = (P("ifg", "tile", None), P(), P(None, "ifg"), P(), P())
    out_specs = (P(None, "tile", "ifg"), P("tile", "ifg"))
    run = functools.partial(shards, physical=(nx, nz, nc))
    return jax.shard_map(run, mesh=mesh, in_specs=in_specs, out_specs=out_specs, check_vma=False)
```

```python
import functools

import jax
import jax.numpy as jnp
import numpy as np
from jax import lax
from jax.experimental import pallas as pl
from jax.experimental.pallas import tpu as pltpu
from jax.sharding import PartitionSpec as P

EPS = 1e-06
RIDGE = 1.0


def smooth_columns(count, padded):
    days = np.arange(count, dtype=np.float64)
    scaled = 2.0 * days / (count - 1) - 1.0
    years = days * 12.0 / 365.25
    smooth = np.stack(
        [
            np.ones_like(days),
            scaled,
            scaled**2,
            scaled**3,
            np.sin(2.0 * np.pi * years),
            np.cos(2.0 * np.pi * years),
            np.sin(4.0 * np.pi * years),
            np.cos(4.0 * np.pi * years),
        ]
    )
    return np.pad(smooth, ((0, 0), (0, padded - count))).astype(np.float32)


def fit_operator(smooth, epochs, count):
    steps = epochs.shape[0]
    index = lax.broadcasted_iota(jnp.int32, (steps, smooth.shape[1]), 1)
    which = lax.broadcasted_iota(jnp.int32, (steps, smooth.shape[1]), 0)
    start = jnp.zeros_like(index)
    for e in range(steps):
        start = jnp.where(which == e, epochs[e], start)
    jumps = jnp.where((index >= start) & (index < count), 1.0, 0.0)
    right = jnp.concatenate([smooth, jumps], axis=0)
    terms = right.shape[0]
    normal = lax.dot_general(
        right,
        right,
        (((1,), (1,)), ((), ())),
        precision=lax.Precision.HIGHEST,
        preferred_element_type=jnp.float32,
    )
    line = lax.broadcasted_iota(jnp.int32, (terms, terms), 0)
    left = normal + jnp.where(
        line == lax.broadcasted_iota(jnp.int32, (terms, terms), 1), RIDGE, 0.0
    )
    wide = lax.broadcasted_iota(jnp.int32, right.shape, 0)
    for j in range(terms):
        pivot = left[j : j + 1, j : j + 1]
        left_row = left[j : j + 1, :] / pivot
        right_row = right[j : j + 1, :] / pivot
        factor = left[:, j : j + 1]
        left = jnp.where(line == j, left_row, left - factor * left_row)
        right = jnp.where(wide == j, right_row, right - factor * right_row)
    return right


def incidence_matrix(pairs, count):
    dates = jnp.arange(count, dtype=jnp.int32)
    later = (pairs[:, 1:2] == dates[None, :]).astype(jnp.float32)
    earlier = (pairs[:, 0:1] == dates[None, :]).astype(jnp.float32)
    return later - earlier


MESH = pl.DeviceIdType.MESH
LANES = 128


def reference_counts(region, tile, rows, width):
    blocks = width // LANES
    line = lax.shift_right_arithmetic(region, width.bit_length() - 1) - tile * rows
    col = lax.bitwise_and(region, width - 1)
    block = lax.shift_right_arithmetic(col, LANES.bit_length() - 1)
    lane = lax.bitwise_and(col, LANES - 1)
    key = jnp.where((line >= 0) & (line < rows), block * rows + line, -1)
    listed = region.shape[1]
    spots = lax.broadcasted_iota(jnp.int32, (blocks * rows, listed), 0) == key
    lanes = lax.broadcasted_iota(jnp.int32, (LANES, listed), 0) == lane
    return lax.dot_general(
        jnp.where(spots, 1.0, 0.0),
        jnp.where(lanes, 1.0, 0.0),
        (((1,), (1,)), ((), ())),
        preferred_element_type=jnp.float32,
    )


def exchange(
    dims, epochs, ifgs, inverse, region, smooth,
    moved, gathered, fit,
    sent, piece, column, counts, local, sums, sem,
):
    nx, nz, nc, tiles = dims
    group = nx * nz * nc
    half = nz // 2
    tile = lax.axis_index("tile")
    me = lax.axis_index("ifg")
    my_c = lax.rem(me, nc)
    my_z = lax.rem(lax.div(me, nc), nz)
    my_x = lax.div(me, nc * nz)

    def place(step):
        plane = lax.div(step, nx * nc)
        inner = lax.rem(step, nx * nc)
        j = lax.div(plane + 1, 2)
        odd = lax.rem(plane, 2)
        dz = odd * (half - j) + (1 - odd) * (half + j)
        dx = nx - 1 - lax.div(inner, nc)
        dc = nc - 1 - lax.rem(inner, nc)
        return lax.rem(my_x + dx, nx), lax.rem(my_z + dz, nz), lax.rem(my_c + dc, nc)

    def device(x, z, c):
        return {"ifg": (x * nz + z) * nc + c, "tile": tile}

    column[...] = jnp.zeros_like(column)
    barrier = pltpu.get_barrier_semaphore()

    def greet(step, carry):
        pl.semaphore_signal(
            barrier, inc=1, device_id=device(*place(step)), device_id_type=MESH
        )
        return carry

    lax.fori_loop(0, group - 1, greet, 0)
    for d in range(1, tiles):
        pl.semaphore_signal(
            barrier,
            inc=1,
            device_id={"ifg": me, "tile": lax.rem(tile + d, tiles)},
            device_id_type=MESH,
        )

    count, rows, width = ifgs.shape
    dates = inverse.shape[1]
    piece[...] = jnp.zeros_like(piece)
    last = -(-dates // LANES) - 1
    for q in range(last + 1):
        lo, hi = q * LANES, min(q * LANES + LANES, dates)

        @pl.when(tile == q)
        def _(lo=lo, hi=hi):
            piece[:count, : hi - lo] = inverse[:, lo:hi]

    column[my_z] = piece[...]
    pieces = last + 1

    counts[...] = reference_counts(region[...], tile, rows, width)

    def collect(block, total):
        col = pl.multiple_of(block * LANES, LANES)
        values = ifgs[:, :, pl.ds(col, LANES)].astype(jnp.float32)
        return total + values * counts[pl.ds(block * rows, rows), :][None]

    local[...] = lax.fori_loop(
        0, width // LANES, collect, jnp.zeros((count, rows, LANES), jnp.float32)
    )
    pl.semaphore_wait(barrier, group - 1 + tiles - 1)

    def partial_copy(d):
        return pltpu.make_async_remote_copy(
            src_ref=local,
            dst_ref=sums.at[d - 1],
            send_sem=sem.at[d],
            recv_sem=sem.at[tiles + d],
            device_id={"ifg": me, "tile": lax.rem(tile + d, tiles)},
            device_id_type=MESH,
        )

    for d in range(1, tiles):
        partial_copy(d).start()

    base = 2 * tiles
    even = -(-count // 2) * 2

    def z_copy(dz, ref):
        return pltpu.make_async_remote_copy(
            src_ref=ref,
            dst_ref=column.at[my_z, pl.ds(0, even)],
            send_sem=sem.at[base],
            recv_sem=sem.at[base + 1],
            device_id=device(my_x, lax.rem(my_z + dz, nz), my_c),
            device_id_type=MESH,
        )

    def send_z(i, carry):
        j = lax.div(i + 1, 2)
        odd = lax.rem(i, 2)
        z_copy(odd * (half - j) + (1 - odd) * (half + j), piece.at[pl.ds(0, even)]).start()
        return carry

    @pl.when(tile < pieces)
    def _():
        lax.fori_loop(0, nz - 1, send_z, 0)


    for d in range(1, tiles):
        partial_copy(d).wait()
    total = local[...]
    for d in range(1, tiles):
        total = total + sums[d - 1]
    mean = jnp.sum(total, axis=(1, 2), keepdims=True) / region.shape[1]
    mean = jnp.broadcast_to(mean, (count, rows, LANES))

    def corrected(x, z, c):
        col = ((x * nz + z) * nc + c) * LANES
        values = ifgs[:, :, pl.ds(pl.multiple_of(col, LANES), LANES)].astype(jnp.float32)
        return (values - mean).astype(jnp.bfloat16)

    def prepare(step, carry):
        sent[step] = corrected(*place(step))
        return carry

    def block_copy(step):
        return pltpu.make_async_remote_copy(
            src_ref=sent.at[step],
            dst_ref=moved.at[my_c, my_x, my_z],
            send_sem=sem.at[base + 2],
            recv_sem=sem.at[base + 3],
            device_id=device(*place(step)),
            device_id_type=MESH,
        )

    def send_block(step, carry):
        block_copy(step).start()
        return carry

    plane = nx * nc
    first = plane * 5
    lax.fori_loop(0, plane, prepare, 0)

    def both(step, carry):
        send_block(step, carry)
        return prepare(step + plane, carry)

    lax.fori_loop(0, first, both, 0)

    arrived = pltpu.make_async_remote_copy(
        src_ref=column.at[pl.ds(0, nz - 1), pl.ds(0, even)],
        dst_ref=column.at[pl.ds(0, nz - 1), pl.ds(0, even)],
        send_sem=sem.at[base],
        recv_sem=sem.at[base + 1],
        device_id=device(my_x, lax.rem(my_z + 1, nz), my_c),
        device_id_type=MESH,
    )
    lanes = pl.ds(pl.multiple_of(jnp.minimum(tile, last) * LANES, LANES), LANES)

    @pl.when(tile < pieces)
    def _():
        arrived.wait()
        tall = column.shape[1]
        target = lax.broadcasted_iota(jnp.int32, (nz * count, nz * tall), 0)
        source = lax.broadcasted_iota(jnp.int32, (nz * count, nz * tall), 1)
        line = lax.bitwise_and(source, tall - 1)
        block = lax.shift_right_arithmetic(source, tall.bit_length() - 1)
        pick = jnp.where((line < count) & (block * count + line == target), 1.0, 0.0)
        gathered[my_c, my_x, :, lanes] = jnp.dot(
            pick.astype(jnp.bfloat16),
            column[...].reshape(nz * tall, LANES),
            preferred_element_type=jnp.float32,
        ).astype(jnp.bfloat16)

    second = first + 2 * plane
    lax.fori_loop(first, second, both, 0)

    def x_copy(d):
        return pltpu.make_async_remote_copy(
            src_ref=gathered.at[my_c, my_x, :, lanes],
            dst_ref=gathered.at[my_c, my_x, :, lanes],
            send_sem=sem.at[base + 2 + 2 * d],
            recv_sem=sem.at[base + 3 + 2 * d],
            device_id=device(lax.rem(my_x + d, nx), my_z, my_c),
            device_id_type=MESH,
        )

    @pl.when(tile < pieces)
    def _():
        for d in range(1, nx):
            x_copy(d).start()

    lax.fori_loop(second, group - 1 - plane, both, 0)
    lax.fori_loop(group - 1 - plane, group - 1, send_block, 0)
    fit[...] = fit_operator(smooth[...], epochs, dates)
    moved[my_c, my_x, my_z] = corrected(my_x, my_z, my_c)

    @pl.when(tile < pieces)
    def _():
        for d in range(1, nx):
            x_copy(d).wait()

    over = base + 2 + 2 * nx

    def tile_copy(d):
        return pltpu.make_async_remote_copy(
            src_ref=gathered.at[my_c, :, :, lanes],
            dst_ref=gathered.at[my_c, :, :, lanes],
            send_sem=sem.at[over + 2 * d],
            recv_sem=sem.at[over + 1 + 2 * d],
            device_id={"ifg": me, "tile": lax.rem(tile + d, tiles)},
            device_id_type=MESH,
        )

    @pl.when(tile < pieces)
    def _():
        for d in range(1, tiles):
            tile_copy(d).start()
        for d in range(1, tiles):
            tile_copy(d).wait_send()

    for d in range(1, tiles):

        @pl.when(lax.rem(tile + tiles - d, tiles) < pieces)
        def _(d=d):
            tile_copy(d).wait_recv()

    core = pltpu.make_async_remote_copy(
        src_ref=gathered.at[my_c],
        dst_ref=gathered.at[my_c],
        send_sem=sem.at[over],
        recv_sem=sem.at[over + 1],
        device_id=device(my_x, my_z, lax.rem(my_c + 1, nc)),
        device_id_type=MESH,
    )
    core.start()
    everything = pltpu.make_async_remote_copy(
        src_ref=sent.at[pl.ds(0, group - 1)],
        dst_ref=sent.at[pl.ds(0, group - 1)],
        send_sem=sem.at[base + 2],
        recv_sem=sem.at[base + 3],
        device_id=device(my_x, lax.rem(my_z + 1, nz), my_c),
        device_id_type=MESH,
    )
    everything.wait()
    core.wait()


def shards(ifgs, pairs, pseudo_inverse, ref_pixels, epochs, physical):
    nx, nz, nc = physical
    count, row_count, col_total = ifgs.shape
    group = lax.axis_size("ifg")
    tiles = lax.axis_size("tile")
    date_count = pseudo_inverse.shape[0]
    padded = -(-date_count // LANES) * LANES
    tall = 16
    vmem = pl.BlockSpec(memory_space=pltpu.VMEM)
    smooth = jnp.asarray(smooth_columns(date_count, padded))
    terms = smooth.shape[0] + epochs.shape[0]
    moved, gathered, fit = pl.pallas_call(
        functools.partial(exchange, (nx, nz, nc, tiles)),
        out_shape=(
            jax.ShapeDtypeStruct((nc, nx, nz, count, row_count, LANES), jnp.bfloat16),
            jax.ShapeDtypeStruct((nc, nx, nz * count, padded), jnp.bfloat16),
            jax.ShapeDtypeStruct((terms, padded), jnp.float32),
        ),
        in_specs=[pl.BlockSpec(memory_space=pltpu.SMEM)] + [vmem] * 4,
        out_specs=(vmem,) * 3,
        scratch_shapes=[
            pltpu.VMEM((group, count, row_count, LANES), jnp.bfloat16),
            pltpu.VMEM((tall, LANES), jnp.bfloat16),
            pltpu.VMEM((nz, tall, LANES), jnp.bfloat16),
            pltpu.VMEM((col_total // LANES * row_count, LANES), jnp.float32),
            pltpu.VMEM((count, row_count, LANES), jnp.float32),
            pltpu.VMEM((tiles - 1, count, row_count, LANES), jnp.float32),
            pltpu.SemaphoreType.DMA((4 * tiles + 2 * nx + 4,)),
        ],
        compiler_params=pltpu.CompilerParams(collective_id=0, has_side_effects=True),
    )(epochs, ifgs, pseudo_inverse.T, ref_pixels[None, :], smooth)
    total = group * count
    pixel_rows = moved.reshape(total, row_count * LANES)
    operator = gathered.reshape(total, padded)
    displacement = lax.dot_general(
        operator,
        pixel_rows,
        (((0,), (0,)), ((), ())),
        preferred_element_type=jnp.float32,
    )
    coeffs = jnp.dot(
        fit, displacement, precision=lax.Precision.HIGHEST, preferred_element_type=jnp.float32
    )
    ordered = pairs.reshape(nx, nz, nc, count, 2).transpose(2, 0, 1, 3, 4).reshape(total, 2)
    incidence = incidence_matrix(ordered, padded)
    predicted = jnp.dot(
        incidence, displacement, precision=lax.Precision.HIGH, preferred_element_type=jnp.float32
    )
    misfit = pixel_rows.astype(jnp.float32) - predicted
    spread = jnp.sqrt(jnp.mean(misfit * misfit, axis=0) + EPS)
    return (
        coeffs.reshape(terms, row_count, LANES),
        spread.reshape(row_count, LANES),
    )


def solution(mesh):
    nx, nc = 4, 2
    nz = mesh.shape["ifg"] // (nx * nc)
    in_specs = (P("ifg", "tile", None), P(), P(None, "ifg"), P(), P())
    out_specs = (P(None, "tile", "ifg"), P("tile", "ifg"))
    run = functools.partial(shards, physical=(nx, nz, nc))
    return jax.shard_map(run, mesh=mesh, in_specs=in_specs, out_specs=out_specs, check_vma=False)
```

```python
import functools

import jax
import jax.numpy as jnp
import numpy as np
from jax import lax
from jax.experimental import pallas as pl
from jax.experimental.pallas import tpu as pltpu
from jax.sharding import PartitionSpec as P

EPS = 1e-06
RIDGE = 1.0


def smooth_columns(count, padded):
    days = np.arange(count, dtype=np.float64)
    scaled = 2.0 * days / (count - 1) - 1.0
    years = days * 12.0 / 365.25
    smooth = np.stack(
        [
            np.ones_like(days),
            scaled,
            scaled**2,
            scaled**3,
            np.sin(2.0 * np.pi * years),
            np.cos(2.0 * np.pi * years),
            np.sin(4.0 * np.pi * years),
            np.cos(4.0 * np.pi * years),
        ]
    )
    return np.pad(smooth, ((0, 0), (0, padded - count))).astype(np.float32)


def fit_operator(smooth, epochs, count):
    steps = epochs.shape[0]
    index = lax.broadcasted_iota(jnp.int32, (steps, smooth.shape[1]), 1)
    which = lax.broadcasted_iota(jnp.int32, (steps, smooth.shape[1]), 0)
    start = jnp.zeros_like(index)
    for e in range(steps):
        start = jnp.where(which == e, epochs[e], start)
    jumps = jnp.where((index >= start) & (index < count), 1.0, 0.0)
    right = jnp.concatenate([smooth, jumps], axis=0)
    terms = right.shape[0]
    normal = lax.dot_general(
        right,
        right,
        (((1,), (1,)), ((), ())),
        precision=lax.Precision.HIGHEST,
        preferred_element_type=jnp.float32,
    )
    line = lax.broadcasted_iota(jnp.int32, (terms, terms), 0)
    left = normal + jnp.where(
        line == lax.broadcasted_iota(jnp.int32, (terms, terms), 1), RIDGE, 0.0
    )
    wide = lax.broadcasted_iota(jnp.int32, right.shape, 0)
    for j in range(terms):
        pivot = left[j : j + 1, j : j + 1]
        left_row = left[j : j + 1, :] / pivot
        right_row = right[j : j + 1, :] / pivot
        factor = left[:, j : j + 1]
        left = jnp.where(line == j, left_row, left - factor * left_row)
        right = jnp.where(wide == j, right_row, right - factor * right_row)
    return right


def incidence_matrix(pairs, count):
    dates = jnp.arange(count, dtype=jnp.int32)
    later = (pairs[:, 1:2] == dates[None, :]).astype(jnp.float32)
    earlier = (pairs[:, 0:1] == dates[None, :]).astype(jnp.float32)
    return later - earlier


MESH = pl.DeviceIdType.MESH
LANES = 128


def reference_counts(region, tile, rows, width):
    blocks = width // LANES
    line = lax.shift_right_arithmetic(region, width.bit_length() - 1) - tile * rows
    col = lax.bitwise_and(region, width - 1)
    block = lax.shift_right_arithmetic(col, LANES.bit_length() - 1)
    lane = lax.bitwise_and(col, LANES - 1)
    key = jnp.where((line >= 0) & (line < rows), block * rows + line, -1)
    listed = region.shape[1]
    spots = lax.broadcasted_iota(jnp.int32, (blocks * rows, listed), 0) == key
    lanes = lax.broadcasted_iota(jnp.int32, (LANES, listed), 0) == lane
    return lax.dot_general(
        jnp.where(spots, 1.0, 0.0),
        jnp.where(lanes, 1.0, 0.0),
        (((1,), (1,)), ((), ())),
        preferred_element_type=jnp.float32,
    )


def exchange(
    dims, epochs, ifgs, inverse, region, smooth,
    moved, gathered, fit,
    sent, piece, column, counts, local, sums, sem,
):
    nx, nz, nc, tiles = dims
    group = nx * nz * nc
    half = nz // 2
    tile = lax.axis_index("tile")
    me = lax.axis_index("ifg")
    my_c = lax.rem(me, nc)
    my_z = lax.rem(lax.div(me, nc), nz)
    my_x = lax.div(me, nc * nz)

    def place(step):
        side = nx * nc
        far = 1 - lax.min(lax.div(step, side), 1)
        later = lax.max(step - side, 0)
        near = lax.div(later, (nz - 2) * side)
        j = lax.div(later, 2 * side) + 1
        within = lax.rem(later, 2 * side)
        odd = lax.rem(within, 2)
        inner = far * step + (1 - far) * ((1 - near) * lax.div(within, 2) + near * within)
        dz = far * half + (1 - far) * (odd * (half - j) + (1 - odd) * (half + j))
        dx = nx - 1 - lax.div(inner, nc)
        dc = nc - 1 - lax.rem(inner, nc)
        return lax.rem(my_x + dx, nx), lax.rem(my_z + dz, nz), lax.rem(my_c + dc, nc)

    def device(x, z, c):
        return {"ifg": (x * nz + z) * nc + c, "tile": tile}

    column[...] = jnp.zeros_like(column)
    barrier = pltpu.get_barrier_semaphore()

    def greet(step, carry):
        pl.semaphore_signal(
            barrier, inc=1, device_id=device(*place(step)), device_id_type=MESH
        )
        return carry

    lax.fori_loop(0, group - 1, greet, 0)
    for d in range(1, tiles):
        pl.semaphore_signal(
            barrier,
            inc=1,
            device_id={"ifg": me, "tile": lax.rem(tile + d, tiles)},
            device_id_type=MESH,
        )

    count, rows, width = ifgs.shape
    dates = inverse.shape[1]
    piece[...] = jnp.zeros_like(piece)
    last = -(-dates // LANES) - 1
    for q in range(last + 1):
        lo, hi = q * LANES, min(q * LANES + LANES, dates)

        @pl.when(tile == q)
        def _(lo=lo, hi=hi):
            piece[:count, : hi - lo] = inverse[:, lo:hi]

    column[my_z] = piece[...]
    pieces = last + 1

    counts[...] = reference_counts(region[...], tile, rows, width)

    def collect(block, total):
        col = pl.multiple_of(block * LANES, LANES)
        values = ifgs[:, :, pl.ds(col, LANES)].astype(jnp.float32)
        return total + values * counts[pl.ds(block * rows, rows), :][None]

    local[...] = lax.fori_loop(
        0, width // LANES, collect, jnp.zeros((count, rows, LANES), jnp.float32)
    )
    pl.semaphore_wait(barrier, group - 1 + tiles - 1)

    def partial_copy(d):
        return pltpu.make_async_remote_copy(
            src_ref=local,
            dst_ref=sums.at[d - 1],
            send_sem=sem.at[d],
            recv_sem=sem.at[tiles + d],
            device_id={"ifg": me, "tile": lax.rem(tile + d, tiles)},
            device_id_type=MESH,
        )

    for d in range(1, tiles):
        partial_copy(d).start()

    base = 2 * tiles
    even = -(-count // 2) * 2

    def z_copy(dz, ref):
        return pltpu.make_async_remote_copy(
            src_ref=ref,
            dst_ref=column.at[my_z, pl.ds(0, even)],
            send_sem=sem.at[base],
            recv_sem=sem.at[base + 1],
            device_id=device(my_x, lax.rem(my_z + dz, nz), my_c),
            device_id_type=MESH,
        )

    def send_z(i, carry):
        j = lax.div(i + 1, 2)
        odd = lax.rem(i, 2)
        z_copy(odd * (half - j) + (1 - odd) * (half + j), piece.at[pl.ds(0, even)]).start()
        return carry

    @pl.when(tile < pieces)
    def _():
        lax.fori_loop(0, nz - 1, send_z, 0)


    for d in range(1, tiles):
        partial_copy(d).wait()
    total = local[...]
    for d in range(1, tiles):
        total = total + sums[d - 1]
    mean = jnp.sum(total, axis=(1, 2), keepdims=True) / region.shape[1]
    mean = jnp.broadcast_to(mean, (count, rows, LANES))

    def corrected(x, z, c):
        col = ((x * nz + z) * nc + c) * LANES
        values = ifgs[:, :, pl.ds(pl.multiple_of(col, LANES), LANES)].astype(jnp.float32)
        return (values - mean).astype(jnp.bfloat16)

    def prepare(step, carry):
        sent[step] = corrected(*place(step))
        return carry

    def block_copy(step):
        return pltpu.make_async_remote_copy(
            src_ref=sent.at[step],
            dst_ref=moved.at[my_c, my_x, my_z],
            send_sem=sem.at[base + 2],
            recv_sem=sem.at[base + 3],
            device_id=device(*place(step)),
            device_id_type=MESH,
        )

    def send_block(step, carry):
        block_copy(step).start()
        return carry

    plane = nx * nc
    first = plane * 5
    lax.fori_loop(0, plane, prepare, 0)

    def both(step, carry):
        send_block(step, carry)
        return prepare(step + plane, carry)

    lax.fori_loop(0, first, both, 0)

    arrived = pltpu.make_async_remote_copy(
        src_ref=column.at[pl.ds(0, nz - 1), pl.ds(0, even)],
        dst_ref=column.at[pl.ds(0, nz - 1), pl.ds(0, even)],
        send_sem=sem.at[base],
        recv_sem=sem.at[base + 1],
        device_id=device(my_x, lax.rem(my_z + 1, nz), my_c),
        device_id_type=MESH,
    )
    lanes = pl.ds(pl.multiple_of(jnp.minimum(tile, last) * LANES, LANES), LANES)

    @pl.when(tile < pieces)
    def _():
        arrived.wait()
        tall = column.shape[1]
        target = lax.broadcasted_iota(jnp.int32, (nz * count, nz * tall), 0)
        source = lax.broadcasted_iota(jnp.int32, (nz * count, nz * tall), 1)
        line = lax.bitwise_and(source, tall - 1)
        block = lax.shift_right_arithmetic(source, tall.bit_length() - 1)
        pick = jnp.where((line < count) & (block * count + line == target), 1.0, 0.0)
        gathered[my_c, my_x, :, lanes] = jnp.dot(
            pick.astype(jnp.bfloat16),
            column[...].reshape(nz * tall, LANES),
            preferred_element_type=jnp.float32,
        ).astype(jnp.bfloat16)

    second = first + 2 * plane
    lax.fori_loop(first, second, both, 0)

    def x_copy(d):
        return pltpu.make_async_remote_copy(
            src_ref=gathered.at[my_c, my_x, :, lanes],
            dst_ref=gathered.at[my_c, my_x, :, lanes],
            send_sem=sem.at[base + 2 + 2 * d],
            recv_sem=sem.at[base + 3 + 2 * d],
            device_id=device(lax.rem(my_x + d, nx), my_z, my_c),
            device_id_type=MESH,
        )

    @pl.when(tile < pieces)
    def _():
        for d in range(1, nx):
            x_copy(d).start()

    lax.fori_loop(second, group - 1 - plane, both, 0)
    lax.fori_loop(group - 1 - plane, group - 1, send_block, 0)
    fit[...] = fit_operator(smooth[...], epochs, dates)
    moved[my_c, my_x, my_z] = corrected(my_x, my_z, my_c)

    @pl.when(tile < pieces)
    def _():
        for d in range(1, nx):
            x_copy(d).wait()

    over = base + 2 + 2 * nx

    def tile_copy(d):
        return pltpu.make_async_remote_copy(
            src_ref=gathered.at[my_c, :, :, lanes],
            dst_ref=gathered.at[my_c, :, :, lanes],
            send_sem=sem.at[over + 2 * d],
            recv_sem=sem.at[over + 1 + 2 * d],
            device_id={"ifg": me, "tile": lax.rem(tile + d, tiles)},
            device_id_type=MESH,
        )

    @pl.when(tile < pieces)
    def _():
        for d in range(1, tiles):
            tile_copy(d).start()
        for d in range(1, tiles):
            tile_copy(d).wait_send()

    for d in range(1, tiles):

        @pl.when(lax.rem(tile + tiles - d, tiles) < pieces)
        def _(d=d):
            tile_copy(d).wait_recv()

    core = pltpu.make_async_remote_copy(
        src_ref=gathered.at[my_c],
        dst_ref=gathered.at[my_c],
        send_sem=sem.at[over],
        recv_sem=sem.at[over + 1],
        device_id=device(my_x, my_z, lax.rem(my_c + 1, nc)),
        device_id_type=MESH,
    )
    core.start()
    everything = pltpu.make_async_remote_copy(
        src_ref=sent.at[pl.ds(0, group - 1)],
        dst_ref=sent.at[pl.ds(0, group - 1)],
        send_sem=sem.at[base + 2],
        recv_sem=sem.at[base + 3],
        device_id=device(my_x, lax.rem(my_z + 1, nz), my_c),
        device_id_type=MESH,
    )
    everything.wait()
    core.wait()


def shards(ifgs, pairs, pseudo_inverse, ref_pixels, epochs, physical):
    nx, nz, nc = physical
    count, row_count, col_total = ifgs.shape
    group = lax.axis_size("ifg")
    tiles = lax.axis_size("tile")
    date_count = pseudo_inverse.shape[0]
    padded = -(-date_count // LANES) * LANES
    tall = 16
    vmem = pl.BlockSpec(memory_space=pltpu.VMEM)
    smooth = jnp.asarray(smooth_columns(date_count, padded))
    terms = smooth.shape[0] + epochs.shape[0]
    moved, gathered, fit = pl.pallas_call(
        functools.partial(exchange, (nx, nz, nc, tiles)),
        out_shape=(
            pltpu.VMEM((nc, nx, nz, count, row_count, LANES), jnp.bfloat16),
            pltpu.VMEM((nc, nx, nz * count, padded), jnp.bfloat16),
            jax.ShapeDtypeStruct((terms, padded), jnp.float32),
        ),
        in_specs=[pl.BlockSpec(memory_space=pltpu.SMEM)] + [vmem] * 4,
        out_specs=(vmem,) * 3,
        scratch_shapes=[
            pltpu.VMEM((group, count, row_count, LANES), jnp.bfloat16),
            pltpu.VMEM((tall, LANES), jnp.bfloat16),
            pltpu.VMEM((nz, tall, LANES), jnp.bfloat16),
            pltpu.VMEM((col_total // LANES * row_count, LANES), jnp.float32),
            pltpu.VMEM((count, row_count, LANES), jnp.float32),
            pltpu.VMEM((tiles - 1, count, row_count, LANES), jnp.float32),
            pltpu.SemaphoreType.DMA((4 * tiles + 2 * nx + 4,)),
        ],
        compiler_params=pltpu.CompilerParams(collective_id=0, has_side_effects=True),
    )(epochs, ifgs, pseudo_inverse.T, ref_pixels[None, :], smooth)
    total = group * count
    pixel_rows = moved.reshape(total, row_count * LANES)
    operator = gathered.reshape(total, padded)
    displacement = lax.dot_general(
        operator,
        pixel_rows,
        (((0,), (0,)), ((), ())),
        preferred_element_type=jnp.float32,
    )
    coeffs = jnp.dot(
        fit, displacement, precision=lax.Precision.HIGHEST, preferred_element_type=jnp.float32
    )
    ordered = pairs.reshape(nx, nz, nc, count, 2).transpose(2, 0, 1, 3, 4).reshape(total, 2)
    incidence = incidence_matrix(ordered, padded)
    predicted = jnp.dot(
        incidence, displacement, precision=lax.Precision.HIGH, preferred_element_type=jnp.float32
    )
    misfit = pixel_rows.astype(jnp.float32) - predicted
    spread = jnp.sqrt(jnp.mean(misfit * misfit, axis=0) + EPS)
    return (
        coeffs.reshape(terms, row_count, LANES),
        spread.reshape(row_count, LANES),
    )


def solution(mesh):
    nx, nc = 4, 2
    nz = mesh.shape["ifg"] // (nx * nc)
    in_specs = (P("ifg", "tile", None), P(), P(None, "ifg"), P(), P())
    out_specs = (P(None, "tile", "ifg"), P("tile", "ifg"))
    run = functools.partial(shards, physical=(nx, nz, nc))
    return jax.shard_map(run, mesh=mesh, in_specs=in_specs, out_specs=out_specs, check_vma=False)
```

```python
import functools

import jax
import jax.numpy as jnp
import numpy as np
from jax import lax
from jax.experimental import pallas as pl
from jax.experimental.pallas import tpu as pltpu
from jax.sharding import PartitionSpec as P

EPS = 1e-06
RIDGE = 1.0


def smooth_columns(count, padded):
    days = np.arange(count, dtype=np.float64)
    scaled = 2.0 * days / (count - 1) - 1.0
    years = days * 12.0 / 365.25
    smooth = np.stack(
        [
            np.ones_like(days),
            scaled,
            scaled**2,
            scaled**3,
            np.sin(2.0 * np.pi * years),
            np.cos(2.0 * np.pi * years),
            np.sin(4.0 * np.pi * years),
            np.cos(4.0 * np.pi * years),
        ]
    )
    return np.pad(smooth, ((0, 0), (0, padded - count))).astype(np.float32)


def fit_operator(smooth, epochs, count):
    steps = epochs.shape[1]
    index = lax.broadcasted_iota(jnp.int32, (steps, smooth.shape[1]), 1)
    which = lax.broadcasted_iota(jnp.int32, (steps, smooth.shape[1]), 0)
    start = jnp.zeros_like(index)
    for e in range(steps):
        start = jnp.where(which == e, epochs[:, e : e + 1], start)
    jumps = jnp.where((index >= start) & (index < count), 1.0, 0.0)
    right = jnp.concatenate([smooth, jumps], axis=0)
    terms = right.shape[0]
    normal = lax.dot_general(
        right,
        right,
        (((1,), (1,)), ((), ())),
        precision=lax.Precision.HIGHEST,
        preferred_element_type=jnp.float32,
    )
    line = lax.broadcasted_iota(jnp.int32, (terms, terms), 0)
    left = normal + jnp.where(
        line == lax.broadcasted_iota(jnp.int32, (terms, terms), 1), RIDGE, 0.0
    )
    wide = lax.broadcasted_iota(jnp.int32, right.shape, 0)
    for j in range(terms):
        pivot = left[j : j + 1, j : j + 1]
        left_row = left[j : j + 1, :] / pivot
        right_row = right[j : j + 1, :] / pivot
        factor = left[:, j : j + 1]
        left = jnp.where(line == j, left_row, left - factor * left_row)
        right = jnp.where(wide == j, right_row, right - factor * right_row)
    return right


def incidence_matrix(pairs, count):
    dates = jnp.arange(count, dtype=jnp.int32)
    later = (pairs[:, 1:2] == dates[None, :]).astype(jnp.float32)
    earlier = (pairs[:, 0:1] == dates[None, :]).astype(jnp.float32)
    return later - earlier


MESH = pl.DeviceIdType.MESH
LANES = 128


def reference_counts(region, tile, rows, width):
    blocks = width // LANES
    line = lax.shift_right_arithmetic(region, width.bit_length() - 1) - tile * rows
    col = lax.bitwise_and(region, width - 1)
    block = lax.shift_right_arithmetic(col, LANES.bit_length() - 1)
    lane = lax.bitwise_and(col, LANES - 1)
    key = jnp.where((line >= 0) & (line < rows), block * rows + line, -1)
    listed = region.shape[1]
    spots = lax.broadcasted_iota(jnp.int32, (blocks * rows, listed), 0) == key
    lanes = lax.broadcasted_iota(jnp.int32, (LANES, listed), 0) == lane
    return lax.dot_general(
        jnp.where(spots, 1.0, 0.0),
        jnp.where(lanes, 1.0, 0.0),
        (((1,), (1,)), ((), ())),
        preferred_element_type=jnp.float32,
    )


def exchange(
    dims, *refs,
):
    far_refs, (moved, gathered, fit), rest = refs[:5], refs[5:8], refs[8:]
    near_refs = rest[:5]
    epochs, ifgs, inverse, region, smooth = near_refs
    (
    sent, piece, column, counts, local, sums, sem,
    ) = rest[5:]
    nx, nz, nc, tiles = dims
    group = nx * nz * nc
    half = nz // 2
    tile = lax.axis_index("tile")
    me = lax.axis_index("ifg")
    my_c = lax.rem(me, nc)
    my_z = lax.rem(lax.div(me, nc), nz)
    my_x = lax.div(me, nc * nz)

    def place(step):
        side = nx * nc
        far = 1 - lax.min(lax.div(step, side), 1)
        later = lax.max(step - side, 0)
        near = lax.div(later, (nz - 2) * side)
        j = lax.div(later, 2 * side) + 1
        within = lax.rem(later, 2 * side)
        odd = lax.rem(within, 2)
        inner = far * step + (1 - far) * ((1 - near) * lax.div(within, 2) + near * within)
        dz = far * half + (1 - far) * (odd * (half - j) + (1 - odd) * (half + j))
        dx = nx - 1 - lax.div(inner, nc)
        dc = nc - 1 - lax.rem(inner, nc)
        return lax.rem(my_x + dx, nx), lax.rem(my_z + dz, nz), lax.rem(my_c + dc, nc)

    def device(x, z, c):
        return {"ifg": (x * nz + z) * nc + c, "tile": tile}

    last_sem = sem.shape[0] - 5
    loads = [
        pltpu.make_async_copy(source, target, sem.at[last_sem + i])
        for i, (source, target) in enumerate(zip(far_refs, near_refs))
    ]
    for load in loads:
        load.start()
    column[...] = jnp.zeros_like(column)
    barrier = pltpu.get_barrier_semaphore()

    def greet(step, carry):
        pl.semaphore_signal(
            barrier, inc=1, device_id=device(*place(step)), device_id_type=MESH
        )
        return carry

    lax.fori_loop(0, group - 1, greet, 0)
    for d in range(1, tiles):
        pl.semaphore_signal(
            barrier,
            inc=1,
            device_id={"ifg": me, "tile": lax.rem(tile + d, tiles)},
            device_id_type=MESH,
        )

    count, rows, width = ifgs.shape
    dates = inverse.shape[1]
    for load in loads:
        load.wait()
    piece[...] = jnp.zeros_like(piece)
    last = -(-dates // LANES) - 1
    for q in range(last + 1):
        lo, hi = q * LANES, min(q * LANES + LANES, dates)

        @pl.when(tile == q)
        def _(lo=lo, hi=hi):
            piece[:count, : hi - lo] = inverse[:, lo:hi]

    column[my_z] = piece[...]
    pieces = last + 1

    counts[...] = reference_counts(region[...], tile, rows, width)

    def collect(block, total):
        col = pl.multiple_of(block * LANES, LANES)
        values = ifgs[:, :, pl.ds(col, LANES)].astype(jnp.float32)
        return total + values * counts[pl.ds(block * rows, rows), :][None]

    local[...] = lax.fori_loop(
        0, width // LANES, collect, jnp.zeros((count, rows, LANES), jnp.float32)
    )
    pl.semaphore_wait(barrier, group - 1 + tiles - 1)

    def partial_copy(d):
        return pltpu.make_async_remote_copy(
            src_ref=local,
            dst_ref=sums.at[d - 1],
            send_sem=sem.at[d],
            recv_sem=sem.at[tiles + d],
            device_id={"ifg": me, "tile": lax.rem(tile + d, tiles)},
            device_id_type=MESH,
        )

    for d in range(1, tiles):
        partial_copy(d).start()

    base = 2 * tiles
    even = -(-count // 2) * 2

    def z_copy(dz, ref):
        return pltpu.make_async_remote_copy(
            src_ref=ref,
            dst_ref=column.at[my_z, pl.ds(0, even)],
            send_sem=sem.at[base],
            recv_sem=sem.at[base + 1],
            device_id=device(my_x, lax.rem(my_z + dz, nz), my_c),
            device_id_type=MESH,
        )

    def send_z(i, carry):
        j = lax.div(i + 1, 2)
        odd = lax.rem(i, 2)
        z_copy(odd * (half - j) + (1 - odd) * (half + j), piece.at[pl.ds(0, even)]).start()
        return carry

    @pl.when(tile < pieces)
    def _():
        lax.fori_loop(0, nz - 1, send_z, 0)


    for d in range(1, tiles):
        partial_copy(d).wait()
    total = local[...]
    for d in range(1, tiles):
        total = total + sums[d - 1]
    mean = jnp.sum(total, axis=(1, 2), keepdims=True) / region.shape[1]
    mean = jnp.broadcast_to(mean, (count, rows, LANES))

    def corrected(x, z, c):
        col = ((x * nz + z) * nc + c) * LANES
        values = ifgs[:, :, pl.ds(pl.multiple_of(col, LANES), LANES)].astype(jnp.float32)
        return (values - mean).astype(jnp.bfloat16)

    def prepare(step, carry):
        sent[step] = corrected(*place(step))
        return carry

    def block_copy(step):
        return pltpu.make_async_remote_copy(
            src_ref=sent.at[step],
            dst_ref=moved.at[my_c, my_x, my_z],
            send_sem=sem.at[base + 2],
            recv_sem=sem.at[base + 3],
            device_id=device(*place(step)),
            device_id_type=MESH,
        )

    def send_block(step, carry):
        block_copy(step).start()
        return carry

    plane = nx * nc
    first = plane * 5
    lax.fori_loop(0, plane, prepare, 0)

    def both(step, carry):
        send_block(step, carry)
        return prepare(step + plane, carry)

    lax.fori_loop(0, first, both, 0)

    arrived = pltpu.make_async_remote_copy(
        src_ref=column.at[pl.ds(0, nz - 1), pl.ds(0, even)],
        dst_ref=column.at[pl.ds(0, nz - 1), pl.ds(0, even)],
        send_sem=sem.at[base],
        recv_sem=sem.at[base + 1],
        device_id=device(my_x, lax.rem(my_z + 1, nz), my_c),
        device_id_type=MESH,
    )
    lanes = pl.ds(pl.multiple_of(jnp.minimum(tile, last) * LANES, LANES), LANES)

    @pl.when(tile < pieces)
    def _():
        arrived.wait()
        tall = column.shape[1]
        target = lax.broadcasted_iota(jnp.int32, (nz * count, nz * tall), 0)
        source = lax.broadcasted_iota(jnp.int32, (nz * count, nz * tall), 1)
        line = lax.bitwise_and(source, tall - 1)
        block = lax.shift_right_arithmetic(source, tall.bit_length() - 1)
        pick = jnp.where((line < count) & (block * count + line == target), 1.0, 0.0)
        gathered[my_c, my_x, :, lanes] = jnp.dot(
            pick.astype(jnp.bfloat16),
            column[...].reshape(nz * tall, LANES),
            preferred_element_type=jnp.float32,
        ).astype(jnp.bfloat16)

    second = first + 2 * plane
    lax.fori_loop(first, second, both, 0)

    def x_copy(d):
        return pltpu.make_async_remote_copy(
            src_ref=gathered.at[my_c, my_x, :, lanes],
            dst_ref=gathered.at[my_c, my_x, :, lanes],
            send_sem=sem.at[base + 2 + 2 * d],
            recv_sem=sem.at[base + 3 + 2 * d],
            device_id=device(lax.rem(my_x + d, nx), my_z, my_c),
            device_id_type=MESH,
        )

    @pl.when(tile < pieces)
    def _():
        for d in range(1, nx):
            x_copy(d).start()

    lax.fori_loop(second, group - 1 - plane, both, 0)
    lax.fori_loop(group - 1 - plane, group - 1, send_block, 0)
    fit[...] = fit_operator(smooth[...], epochs[...], dates)
    moved[my_c, my_x, my_z] = corrected(my_x, my_z, my_c)

    @pl.when(tile < pieces)
    def _():
        for d in range(1, nx):
            x_copy(d).wait()

    over = base + 2 + 2 * nx

    def tile_copy(d):
        return pltpu.make_async_remote_copy(
            src_ref=gathered.at[my_c, :, :, lanes],
            dst_ref=gathered.at[my_c, :, :, lanes],
            send_sem=sem.at[over + 2 * d],
            recv_sem=sem.at[over + 1 + 2 * d],
            device_id={"ifg": me, "tile": lax.rem(tile + d, tiles)},
            device_id_type=MESH,
        )

    @pl.when(tile < pieces)
    def _():
        for d in range(1, tiles):
            tile_copy(d).start()
        for d in range(1, tiles):
            tile_copy(d).wait_send()

    for d in range(1, tiles):

        @pl.when(lax.rem(tile + tiles - d, tiles) < pieces)
        def _(d=d):
            tile_copy(d).wait_recv()

    core = pltpu.make_async_remote_copy(
        src_ref=gathered.at[my_c],
        dst_ref=gathered.at[my_c],
        send_sem=sem.at[over],
        recv_sem=sem.at[over + 1],
        device_id=device(my_x, my_z, lax.rem(my_c + 1, nc)),
        device_id_type=MESH,
    )
    core.start()
    everything = pltpu.make_async_remote_copy(
        src_ref=sent.at[pl.ds(0, group - 1)],
        dst_ref=sent.at[pl.ds(0, group - 1)],
        send_sem=sem.at[base + 2],
        recv_sem=sem.at[base + 3],
        device_id=device(my_x, lax.rem(my_z + 1, nz), my_c),
        device_id_type=MESH,
    )
    everything.wait()
    core.wait()


def shards(ifgs, pairs, pseudo_inverse, ref_pixels, epochs, physical):
    nx, nz, nc = physical
    count, row_count, col_total = ifgs.shape
    group = lax.axis_size("ifg")
    tiles = lax.axis_size("tile")
    date_count = pseudo_inverse.shape[0]
    padded = -(-date_count // LANES) * LANES
    tall = 16
    vmem = pl.BlockSpec(memory_space=pltpu.VMEM)
    smooth = jnp.asarray(smooth_columns(date_count, padded))
    terms = smooth.shape[0] + epochs.shape[0]
    operands = (epochs[None, :], ifgs, pseudo_inverse.T, ref_pixels[None, :], smooth)
    moved, gathered, fit = pl.pallas_call(
        functools.partial(exchange, (nx, nz, nc, tiles)),
        out_shape=(
            pltpu.VMEM((nc, nx, nz, count, row_count, LANES), jnp.bfloat16),
            pltpu.VMEM((nc, nx, nz * count, padded), jnp.bfloat16),
            pltpu.VMEM((terms, padded), jnp.float32),
        ),
        in_specs=[pl.BlockSpec(memory_space=pltpu.HBM)] * 5,
        out_specs=(vmem,) * 3,
        scratch_shapes=[pltpu.VMEM(a.shape, a.dtype) for a in operands]
        + [
            pltpu.VMEM((group, count, row_count, LANES), jnp.bfloat16),
            pltpu.VMEM((tall, LANES), jnp.bfloat16),
            pltpu.VMEM((nz, tall, LANES), jnp.bfloat16),
            pltpu.VMEM((col_total // LANES * row_count, LANES), jnp.float32),
            pltpu.VMEM((count, row_count, LANES), jnp.float32),
            pltpu.VMEM((tiles - 1, count, row_count, LANES), jnp.float32),
            pltpu.SemaphoreType.DMA((4 * tiles + 2 * nx + 9,)),
        ],
        compiler_params=pltpu.CompilerParams(collective_id=0, has_side_effects=True),
    )(*operands)
    total = group * count
    pixel_rows = moved.reshape(total, row_count * LANES)
    operator = gathered.reshape(total, padded)
    displacement = lax.dot_general(
        operator,
        pixel_rows,
        (((0,), (0,)), ((), ())),
        preferred_element_type=jnp.float32,
    )
    coeffs = jnp.dot(
        fit, displacement, precision=lax.Precision.HIGHEST, preferred_element_type=jnp.float32
    )
    ordered = pairs.reshape(nx, nz, nc, count, 2).transpose(2, 0, 1, 3, 4).reshape(total, 2)
    incidence = incidence_matrix(ordered, padded)
    predicted = jnp.dot(
        incidence, displacement, precision=lax.Precision.HIGH, preferred_element_type=jnp.float32
    )
    misfit = pixel_rows.astype(jnp.float32) - predicted
    spread = jnp.sqrt(jnp.mean(misfit * misfit, axis=0) + EPS)
    return (
        coeffs.reshape(terms, row_count, LANES),
        spread.reshape(row_count, LANES),
    )


def solution(mesh):
    nx, nc = 4, 2
    nz = mesh.shape["ifg"] // (nx * nc)
    in_specs = (P("ifg", "tile", None), P(), P(None, "ifg"), P(), P())
    out_specs = (P(None, "tile", "ifg"), P("tile", "ifg"))
    run = functools.partial(shards, physical=(nx, nz, nc))
    return jax.shard_map(run, mesh=mesh, in_specs=in_specs, out_specs=out_specs, check_vma=False)
```

```python
import functools

import jax
import jax.numpy as jnp
import numpy as np
from jax import lax
from jax.experimental import pallas as pl
from jax.experimental.pallas import tpu as pltpu
from jax.sharding import PartitionSpec as P

EPS = 1e-06
RIDGE = 1.0


def smooth_columns(count, padded):
    days = np.arange(count, dtype=np.float64)
    scaled = 2.0 * days / (count - 1) - 1.0
    years = days * 12.0 / 365.25
    smooth = np.stack(
        [
            np.ones_like(days),
            scaled,
            scaled**2,
            scaled**3,
            np.sin(2.0 * np.pi * years),
            np.cos(2.0 * np.pi * years),
            np.sin(4.0 * np.pi * years),
            np.cos(4.0 * np.pi * years),
        ]
    )
    return np.pad(smooth, ((0, 0), (0, padded - count))).astype(np.float32)


def fit_operator(smooth, epochs, count):
    steps = epochs.shape[1]
    index = lax.broadcasted_iota(jnp.int32, (steps, smooth.shape[1]), 1)
    which = lax.broadcasted_iota(jnp.int32, (steps, smooth.shape[1]), 0)
    start = jnp.zeros_like(index)
    for e in range(steps):
        start = jnp.where(which == e, epochs[:, e : e + 1], start)
    jumps = jnp.where((index >= start) & (index < count), 1.0, 0.0)
    right = jnp.concatenate([smooth, jumps], axis=0)
    terms = right.shape[0]
    normal = lax.dot_general(
        right,
        right,
        (((1,), (1,)), ((), ())),
        precision=lax.Precision.HIGHEST,
        preferred_element_type=jnp.float32,
    )
    line = lax.broadcasted_iota(jnp.int32, (terms, terms), 0)
    left = normal + jnp.where(
        line == lax.broadcasted_iota(jnp.int32, (terms, terms), 1), RIDGE, 0.0
    )
    wide = lax.broadcasted_iota(jnp.int32, right.shape, 0)
    for j in range(terms):
        pivot = left[j : j + 1, j : j + 1]
        left_row = left[j : j + 1, :] / pivot
        right_row = right[j : j + 1, :] / pivot
        factor = left[:, j : j + 1]
        left = jnp.where(line == j, left_row, left - factor * left_row)
        right = jnp.where(wide == j, right_row, right - factor * right_row)
    return right


def incidence_matrix(pairs, count):
    dates = jnp.arange(count, dtype=jnp.int32)
    later = (pairs[:, 1:2] == dates[None, :]).astype(jnp.float32)
    earlier = (pairs[:, 0:1] == dates[None, :]).astype(jnp.float32)
    return later - earlier


MESH = pl.DeviceIdType.MESH
LANES = 128


def reference_counts(region, tile, rows, width):
    blocks = width // LANES
    line = lax.shift_right_arithmetic(region, width.bit_length() - 1) - tile * rows
    col = lax.bitwise_and(region, width - 1)
    block = lax.shift_right_arithmetic(col, LANES.bit_length() - 1)
    lane = lax.bitwise_and(col, LANES - 1)
    key = jnp.where((line >= 0) & (line < rows), block * rows + line, -1)
    listed = region.shape[1]
    spots = lax.broadcasted_iota(jnp.int32, (blocks * rows, listed), 0) == key
    lanes = lax.broadcasted_iota(jnp.int32, (LANES, listed), 0) == lane
    return lax.dot_general(
        jnp.where(spots, 1.0, 0.0),
        jnp.where(lanes, 1.0, 0.0),
        (((1,), (1,)), ((), ())),
        preferred_element_type=jnp.float32,
    )


def exchange(
    dims, *refs,
):
    far_refs, (moved, gathered, fit), rest = refs[:5], refs[5:8], refs[8:]
    near_refs = rest[:5]
    epochs, ifgs, inverse, region, smooth = near_refs
    (
    sent, piece, column, counts, local, sums, sem,
    ) = rest[5:]
    nx, nz, nc, tiles = dims
    group = nx * nz * nc
    half = nz // 2
    tile = lax.axis_index("tile")
    me = lax.axis_index("ifg")
    my_c = lax.rem(me, nc)
    my_z = lax.rem(lax.div(me, nc), nz)
    my_x = lax.div(me, nc * nz)

    def place(step):
        side = nx * nc
        far = 1 - lax.min(lax.div(step, side), 1)
        later = lax.max(step - side, 0)
        near = lax.div(later, (nz - 2) * side)
        j = lax.div(later, 2 * side) + 1
        within = lax.rem(later, 2 * side)
        odd = lax.rem(within, 2)
        inner = far * step + (1 - far) * ((1 - near) * lax.div(within, 2) + near * within)
        dz = far * half + (1 - far) * (odd * (half - j) + (1 - odd) * (half + j))
        dx = nx - 1 - lax.div(inner, nc)
        dc = nc - 1 - lax.rem(inner, nc)
        return lax.rem(my_x + dx, nx), lax.rem(my_z + dz, nz), lax.rem(my_c + dc, nc)

    def device(x, z, c):
        return {"ifg": (x * nz + z) * nc + c, "tile": tile}

    last_sem = sem.shape[0] - 5
    loads = [
        pltpu.make_async_copy(source, target, sem.at[last_sem + i])
        for i, (source, target) in enumerate(zip(far_refs, near_refs))
    ]
    for load in loads:
        load.start()
    column[...] = jnp.zeros_like(column)
    barrier = pltpu.get_barrier_semaphore()

    def greet(step, carry):
        peer = {"ifg": lax.rem(me + step, group), "tile": tile}
        pl.semaphore_signal(barrier, inc=1, device_id=peer, device_id_type=MESH)
        return carry

    lax.fori_loop(1, group, greet, 0)
    for d in range(1, tiles):
        pl.semaphore_signal(
            barrier,
            inc=1,
            device_id={"ifg": me, "tile": lax.rem(tile + d, tiles)},
            device_id_type=MESH,
        )

    count, rows, width = ifgs.shape
    dates = inverse.shape[1]
    for load in loads:
        load.wait()
    piece[...] = jnp.zeros_like(piece)
    last = -(-dates // LANES) - 1
    for q in range(last + 1):
        lo, hi = q * LANES, min(q * LANES + LANES, dates)

        @pl.when(tile == q)
        def _(lo=lo, hi=hi):
            piece[:count, : hi - lo] = inverse[:, lo:hi]

    column[my_z] = piece[...]
    pieces = last + 1

    counts[...] = reference_counts(region[...], tile, rows, width)

    def collect(block, total):
        col = pl.multiple_of(block * LANES, LANES)
        values = ifgs[:, :, pl.ds(col, LANES)].astype(jnp.float32)
        return total + values * counts[pl.ds(block * rows, rows), :][None]

    local[...] = lax.fori_loop(
        0, width // LANES, collect, jnp.zeros((count, rows, LANES), jnp.float32)
    )
    pl.semaphore_wait(barrier, group - 1 + tiles - 1)

    def partial_copy(d):
        return pltpu.make_async_remote_copy(
            src_ref=local,
            dst_ref=sums.at[d - 1],
            send_sem=sem.at[d],
            recv_sem=sem.at[tiles + d],
            device_id={"ifg": me, "tile": lax.rem(tile + d, tiles)},
            device_id_type=MESH,
        )

    for d in range(1, tiles):
        partial_copy(d).start()

    base = 2 * tiles
    even = -(-count // 2) * 2

    def z_copy(dz, ref):
        return pltpu.make_async_remote_copy(
            src_ref=ref,
            dst_ref=column.at[my_z, pl.ds(0, even)],
            send_sem=sem.at[base],
            recv_sem=sem.at[base + 1],
            device_id=device(my_x, lax.rem(my_z + dz, nz), my_c),
            device_id_type=MESH,
        )

    def send_z(i, carry):
        j = lax.div(i + 1, 2)
        odd = lax.rem(i, 2)
        z_copy(odd * (half - j) + (1 - odd) * (half + j), piece.at[pl.ds(0, even)]).start()
        return carry

    @pl.when(tile < pieces)
    def _():
        lax.fori_loop(0, nz - 1, send_z, 0)


    for d in range(1, tiles):
        partial_copy(d).wait()
    total = local[...]
    for d in range(1, tiles):
        total = total + sums[d - 1]
    mean = jnp.sum(total, axis=(1, 2), keepdims=True) / region.shape[1]
    mean = jnp.broadcast_to(mean, (count, rows, LANES))

    def corrected(x, z, c):
        col = ((x * nz + z) * nc + c) * LANES
        values = ifgs[:, :, pl.ds(pl.multiple_of(col, LANES), LANES)].astype(jnp.float32)
        return (values - mean).astype(jnp.bfloat16)

    def prepare(step, carry):
        sent[step] = corrected(*place(step))
        return carry

    def block_copy(step):
        return pltpu.make_async_remote_copy(
            src_ref=sent.at[step],
            dst_ref=moved.at[my_c, my_x, my_z],
            send_sem=sem.at[base + 2],
            recv_sem=sem.at[base + 3],
            device_id=device(*place(step)),
            device_id_type=MESH,
        )

    def send_block(step, carry):
        block_copy(step).start()
        return carry

    plane = nx * nc
    first = plane * 5
    lax.fori_loop(0, plane, prepare, 0)

    def both(step, carry):
        send_block(step, carry)
        return prepare(step + plane, carry)

    lax.fori_loop(0, first, both, 0)

    arrived = pltpu.make_async_remote_copy(
        src_ref=column.at[pl.ds(0, nz - 1), pl.ds(0, even)],
        dst_ref=column.at[pl.ds(0, nz - 1), pl.ds(0, even)],
        send_sem=sem.at[base],
        recv_sem=sem.at[base + 1],
        device_id=device(my_x, lax.rem(my_z + 1, nz), my_c),
        device_id_type=MESH,
    )
    lanes = pl.ds(pl.multiple_of(jnp.minimum(tile, last) * LANES, LANES), LANES)

    @pl.when(tile < pieces)
    def _():
        arrived.wait()
        tall = column.shape[1]
        target = lax.broadcasted_iota(jnp.int32, (nz * count, nz * tall), 0)
        source = lax.broadcasted_iota(jnp.int32, (nz * count, nz * tall), 1)
        line = lax.bitwise_and(source, tall - 1)
        block = lax.shift_right_arithmetic(source, tall.bit_length() - 1)
        pick = jnp.where((line < count) & (block * count + line == target), 1.0, 0.0)
        gathered[my_c, my_x, :, lanes] = jnp.dot(
            pick.astype(jnp.bfloat16),
            column[...].reshape(nz * tall, LANES),
            preferred_element_type=jnp.float32,
        ).astype(jnp.bfloat16)

    second = first + 2 * plane
    lax.fori_loop(first, second, both, 0)

    def x_copy(d):
        return pltpu.make_async_remote_copy(
            src_ref=gathered.at[my_c, my_x, :, lanes],
            dst_ref=gathered.at[my_c, my_x, :, lanes],
            send_sem=sem.at[base + 2 + 2 * d],
            recv_sem=sem.at[base + 3 + 2 * d],
            device_id=device(lax.rem(my_x + d, nx), my_z, my_c),
            device_id_type=MESH,
        )

    @pl.when(tile < pieces)
    def _():
        for d in range(1, nx):
            x_copy(d).start()

    lax.fori_loop(second, group - 1 - plane, both, 0)
    lax.fori_loop(group - 1 - plane, group - 1, send_block, 0)
    fit[...] = fit_operator(smooth[...], epochs[...], dates)
    moved[my_c, my_x, my_z] = corrected(my_x, my_z, my_c)

    @pl.when(tile < pieces)
    def _():
        for d in range(1, nx):
            x_copy(d).wait()

    over = base + 2 + 2 * nx

    def tile_copy(d):
        return pltpu.make_async_remote_copy(
            src_ref=gathered.at[my_c, :, :, lanes],
            dst_ref=gathered.at[my_c, :, :, lanes],
            send_sem=sem.at[over + 2 * d],
            recv_sem=sem.at[over + 1 + 2 * d],
            device_id={"ifg": me, "tile": lax.rem(tile + d, tiles)},
            device_id_type=MESH,
        )

    @pl.when(tile < pieces)
    def _():
        for d in range(1, tiles):
            tile_copy(d).start()
        for d in range(1, tiles):
            tile_copy(d).wait_send()

    for d in range(1, tiles):

        @pl.when(lax.rem(tile + tiles - d, tiles) < pieces)
        def _(d=d):
            tile_copy(d).wait_recv()

    core = pltpu.make_async_remote_copy(
        src_ref=gathered.at[my_c],
        dst_ref=gathered.at[my_c],
        send_sem=sem.at[over],
        recv_sem=sem.at[over + 1],
        device_id=device(my_x, my_z, lax.rem(my_c + 1, nc)),
        device_id_type=MESH,
    )
    core.start()
    everything = pltpu.make_async_remote_copy(
        src_ref=sent.at[pl.ds(0, group - 1)],
        dst_ref=sent.at[pl.ds(0, group - 1)],
        send_sem=sem.at[base + 2],
        recv_sem=sem.at[base + 3],
        device_id=device(my_x, lax.rem(my_z + 1, nz), my_c),
        device_id_type=MESH,
    )
    everything.wait()
    core.wait()


def shards(ifgs, pairs, pseudo_inverse, ref_pixels, epochs, physical):
    nx, nz, nc = physical
    count, row_count, col_total = ifgs.shape
    group = lax.axis_size("ifg")
    tiles = lax.axis_size("tile")
    date_count = pseudo_inverse.shape[0]
    padded = -(-date_count // LANES) * LANES
    tall = 16
    vmem = pl.BlockSpec(memory_space=pltpu.VMEM)
    smooth = jnp.asarray(smooth_columns(date_count, padded))
    terms = smooth.shape[0] + epochs.shape[0]
    operands = (epochs[None, :], ifgs, pseudo_inverse.T, ref_pixels[None, :], smooth)
    moved, gathered, fit = pl.pallas_call(
        functools.partial(exchange, (nx, nz, nc, tiles)),
        out_shape=(
            pltpu.VMEM((nc, nx, nz, count, row_count, LANES), jnp.bfloat16),
            pltpu.VMEM((nc, nx, nz * count, padded), jnp.bfloat16),
            pltpu.VMEM((terms, padded), jnp.float32),
        ),
        in_specs=[pl.BlockSpec(memory_space=pltpu.HBM)] * 5,
        out_specs=(vmem,) * 3,
        scratch_shapes=[pltpu.VMEM(a.shape, a.dtype) for a in operands]
        + [
            pltpu.VMEM((group, count, row_count, LANES), jnp.bfloat16),
            pltpu.VMEM((tall, LANES), jnp.bfloat16),
            pltpu.VMEM((nz, tall, LANES), jnp.bfloat16),
            pltpu.VMEM((col_total // LANES * row_count, LANES), jnp.float32),
            pltpu.VMEM((count, row_count, LANES), jnp.float32),
            pltpu.VMEM((tiles - 1, count, row_count, LANES), jnp.float32),
            pltpu.SemaphoreType.DMA((4 * tiles + 2 * nx + 9,)),
        ],
        compiler_params=pltpu.CompilerParams(collective_id=0, has_side_effects=True),
    )(*operands)
    total = group * count
    pixel_rows = moved.reshape(total, row_count * LANES)
    operator = gathered.reshape(total, padded)
    displacement = lax.dot_general(
        operator,
        pixel_rows,
        (((0,), (0,)), ((), ())),
        preferred_element_type=jnp.float32,
    )
    coeffs = jnp.dot(
        fit, displacement, precision=lax.Precision.HIGHEST, preferred_element_type=jnp.float32
    )
    ordered = pairs.reshape(nx, nz, nc, count, 2).transpose(2, 0, 1, 3, 4).reshape(total, 2)
    incidence = incidence_matrix(ordered, padded)
    predicted = jnp.dot(
        incidence, displacement, precision=lax.Precision.HIGH, preferred_element_type=jnp.float32
    )
    misfit = pixel_rows.astype(jnp.float32) - predicted
    spread = jnp.sqrt(jnp.mean(misfit * misfit, axis=0) + EPS)
    return (
        coeffs.reshape(terms, row_count, LANES),
        spread.reshape(row_count, LANES),
    )


def solution(mesh):
    nx, nc = 4, 2
    nz = mesh.shape["ifg"] // (nx * nc)
    in_specs = (P("ifg", "tile", None), P(), P(None, "ifg"), P(), P())
    out_specs = (P(None, "tile", "ifg"), P("tile", "ifg"))
    run = functools.partial(shards, physical=(nx, nz, nc))
    return jax.shard_map(run, mesh=mesh, in_specs=in_specs, out_specs=out_specs, check_vma=False)
```
